32 devices in a mesh: dp: 8 (over y, x, core), seq: 4 (over z).
Axes of the slice: x: 2, y: 2, z: 4, core: 2. Of those that a mesh axis runs over, the one named last changes fastest.
Arguments:
- inputs: bfloat16 [8, 1024, 1088], P('dp', 'seq'), may hold values from -6 to 6
- lengths: int32 [8], P('dp'), may hold values from 1 to 1024, 5734 in all
- cotangent: bfloat16 [8, 1024, 1088], P('dp', 'seq'), may hold values from -6 to 6
- norm1_gain: bfloat16 [1088], P('dp'), may hold values from 0.5 to 1.5
- norm1_bias: bfloat16 [1088], P('dp'), may hold values from -3 to 3
- qkv_weight: bfloat16 [1088, 3264], P('dp', 'seq'), may hold values from -0.1875 to 0.1875
- query_bias: bfloat16 [1088], P('dp'), may hold values from -3 to 3
- value_bias: bfloat16 [1088], P('dp'), may hold values from -3 to 3
- out_weight: bfloat16 [1088, 1088], P('dp', 'seq'), may hold values from -1.5 to 1.5
- out_bias: bfloat16 [1088], P('dp'), may hold values from -3 to 3
- norm2_gain: bfloat16 [1088], P('dp'), may hold values from 0.5 to 1.5
- norm2_bias: bfloat16 [1088], P('dp'), may hold values from -3 to 3
- up_weight: bfloat16 [1088, 4352], P('dp', 'seq'), may hold values from -0.1875 to 0.1875
- up_bias: bfloat16 [4352], P('dp'), may hold values from -3 to 3
- down_weight: bfloat16 [4352, 1088], P('seq', 'dp'), may hold values from -0.09375 to 0.09375
- down_bias: bfloat16 [1088], P('dp'), may hold values from -3 to 3
Outputs:
- outputs: bfloat16 [8, 1024, 1088], P('dp', 'seq')
- input_grad: float32 [8, 1024, 1088], P('dp', 'seq')
- norm1_gain_grad: float32 [1088], P('dp')
- norm1_bias_grad: float32 [1088], P('dp')
- qkv_weight_grad: float32 [1088, 3264], P('dp', 'seq')
- query_bias_grad: float32 [1088], P('dp')
- value_bias_grad: float32 [1088], P('dp')
- out_weight_grad: float32 [1088, 1088], P('dp', 'seq')
- out_bias_grad: float32 [1088], P('dp')
- norm2_gain_grad: float32 [1088], P('dp')
- norm2_bias_grad: float32 [1088], P('dp')
- up_weight_grad: float32 [1088, 4352], P('dp', 'seq')
- up_bias_grad: float32 [4352], P('dp')
- down_weight_grad: float32 [4352, 1088], P('seq', 'dp')
- down_bias_grad: float32 [1088], P('dp')
The draws below stay inside these ranges and needn't reach their ends.
Inputs may be any that keep to these rules, and one draw needn't show every extreme that they name: `lengths`: each of the 8 sequences has its live tokens at the front of its slot, 5734 in all; the longest fills its slot.
All inputs are finite; a program needn't handle non-finite values. No bound on the sum of `lengths` on one device may be relied on, other than what follows from the above.
Results may differ from the reference program's by a relative error of at most 0.011.
Values may be sent and summed in bfloat16 or wider, within the bound.
No kernel may reach another device: no remote copies, remote signals or barrier semaphores. Data moves between devices by JAX's collectives and lax.ppermute only.
A program may use at most 128 MiB of HBM per device.

```python
import math
import jax
import jax.numpy as jnp
import numpy as np
from jax import lax

D = 1088
HEADS = 17
HD = 64
FF = 4352
L = 1024
SEQS = 8
LIVE = 5734


def block_levels(rng, extent, split, low, top_value):
    loudness, own = 1.0, jax.random.fold_in(rng, 6)
    for axis_at, blocks in split:
        steps = jnp.exp(jax.random.uniform(jax.random.fold_in(own, axis_at), (blocks,), jnp.float32, low / len(split), top_value / len(split)))
        loudness = loudness * jnp.repeat(steps, extent[axis_at] // blocks).reshape([-1 if axis == axis_at else 1 for axis in range(len(extent))])
    return loudness


def split_up(count, total, most, slope):
    portions = [(1 << 20) // math.isqrt(rank ** slope) + 1 for rank in range(2, count + 1)]
    surplus, given = total - most - (count - 1), [1] * (count - 1)
    while surplus > 0:
        free = [i for i in range(count - 1) if given[i] < most]
        whole, left = sum([portions[i] for i in free]), surplus
        for i in free:
            addition = min(most - given[i], max(1, left * portions[i] // whole), surplus)
            given[i] = given[i] + addition
            surplus = surplus - addition
    return np.array([most] + given)


def uneven_parts(stream_key, number_of, total, reach, lean):
    if number_of == 2:
        one = jax.random.randint(stream_key, (), max(1, total - reach), min(reach, total - 1) + 1)
        return jnp.stack([one, total - one])
    tallies = jnp.asarray(split_up(number_of, total, reach, lean), jnp.int32)
    twos = (number_of - 1) // 2
    donor, sink = tallies[1:1 + 2 * twos:2], tallies[2:2 + 2 * twos:2]
    room = jnp.minimum(donor - 1, reach - sink)
    shifted = jax.random.randint(jax.random.fold_in(stream_key, 1), (twos,), 0, 1 << 20) % (room + 1)
    tallies = tallies.at[1:1 + 2 * twos:2].set(donor - shifted).at[2:2 + 2 * twos:2].set(sink + shifted)
    return tallies[jax.random.permutation(jax.random.fold_in(stream_key, 2), number_of)]


def normal_values(stream_key, dims, width, most, split=(), kind=jnp.bfloat16):
    array = width * jax.random.normal(stream_key, dims, jnp.float32)
    if split:
        array = array * block_levels(stream_key, dims, split, -0.22, 0.18)
    return jnp.clip(array, -most, most).astype(kind)


def setup_inputs(seed: int = 0) -> dict:
    key_list = jax.random.split(jax.random.key(seed), 17)
    inputs = normal_values(key_list[0], (SEQS, L, D), 1.0, 6.0, ((0, 8), (1, 4)))
    lengths = uneven_parts(key_list[1], SEQS, LIVE, L, 2).astype(jnp.int32)
    cotangent = normal_values(key_list[2], (SEQS, L, D), 1.0, 6.0, ((0, 8), (1, 4)))
    norm1_gain = jnp.clip(1.0 + 0.1 * jax.random.normal(key_list[3], (D,), jnp.float32), 0.5, 1.5).astype(jnp.bfloat16)
    norm1_bias = normal_values(key_list[4], (D,), 0.5, 3.0, ((0, 8),))
    qkv_weight = normal_values(key_list[5], (D, 3 * D), D ** -0.5, 0.1875, ((0, 8), (1, 4)))
    query_bias = normal_values(key_list[6], (D,), 0.5, 3.0, ((0, 8),))
    value_bias = normal_values(key_list[7], (D,), 0.5, 3.0, ((0, 8),))
    out_weight = normal_values(key_list[8], (D, D), (max(D // 64, 1)) ** -0.5, 1.5, ((0, 8), (1, 4)))
    out_bias = normal_values(key_list[9], (D,), 0.5, 3.0, ((0, 8),))
    norm2_gain = jnp.clip(1.0 + 0.1 * jax.random.normal(key_list[10], (D,), jnp.float32), 0.5, 1.5).astype(jnp.bfloat16)
    norm2_bias = normal_values(key_list[11], (D,), 0.5, 3.0, ((0, 8),))
    up_weight = normal_values(key_list[12], (D, FF), D ** -0.5, 0.1875, ((0, 8), (1, 4)))
    up_bias = normal_values(key_list[13], (FF,), 0.5, 3.0, ((0, 8),))
    down_weight = normal_values(key_list[14], (FF, D), FF ** -0.5, 0.09375, ((0, 4), (1, 8)))
    down_bias = normal_values(key_list[15], (D,), 0.5, 3.0, ((0, 8),))
    return dict(inputs=inputs, lengths=lengths, cotangent=cotangent, norm1_gain=norm1_gain, norm1_bias=norm1_bias, qkv_weight=qkv_weight, query_bias=query_bias, value_bias=value_bias, out_weight=out_weight, out_bias=out_bias, norm2_gain=norm2_gain, norm2_bias=norm2_bias, up_weight=up_weight, up_bias=up_bias, down_weight=down_weight, down_bias=down_bias)


norm_eps = 1e-05
gelu_coef = 0.7978845608028654
masked_value = -1e+30

def layer_norm(values, norm_gain, norm_shift):
    average = lax.optimization_barrier(jnp.mean(values, axis=-1, keepdims=True))
    centered = values - average
    variance = lax.optimization_barrier(jnp.mean(centered * centered, axis=-1, keepdims=True))
    inv_std = lax.rsqrt(variance + norm_eps)
    normed = centered * inv_std
    return (normed, inv_std, normed * norm_gain + norm_shift)

def norm_back(grad_in, normed, inv_std, norm_gain):
    scaled = grad_in * norm_gain
    return inv_std * (scaled - lax.optimization_barrier(jnp.mean(scaled, axis=-1, keepdims=True)) - normed * lax.optimization_barrier(jnp.mean(scaled * normed, axis=-1, keepdims=True)))

def gelu_parts(pre_act):
    tangent = jnp.tanh(gelu_coef * (pre_act + 0.044715 * pre_act * pre_act * pre_act))
    result = 0.5 * pre_act * (1.0 + tangent)
    derivative = 0.5 * (1.0 + tangent) + 0.5 * pre_act * (1.0 - tangent * tangent) * gelu_coef * (1.0 + 3.0 * 0.044715 * pre_act * pre_act)
    return (result, derivative)

def split_heads(matrix):
    return matrix.reshape(matrix.shape[0], HEADS, HD).transpose(1, 0, 2)

def merge_heads(stacked):
    return stacked.transpose(1, 0, 2).reshape(stacked.shape[1], HEADS * HD)

def head_scores(query_head, key_head, allowed):
    scaling = query_head.shape[-1] ** (-0.5)
    scores = jnp.dot(query_head, key_head.T, preferred_element_type=jnp.float32) * scaling
    return jnp.where(allowed, scores, masked_value)

def attend(queries, key_rows, value_rows, allowed):

    def per_head(operands):
        query_head, key_head, value_head = operands
        scores = head_scores(query_head, key_head, allowed)
        largest = lax.optimization_barrier(jnp.max(scores, axis=-1, keepdims=True))
        logsum = largest + jnp.log(lax.optimization_barrier(jnp.sum(jnp.exp(scores - largest), axis=-1, keepdims=True)))
        weights = jnp.exp(scores - logsum).astype(jnp.bfloat16)
        context = jnp.dot(weights, value_head, preferred_element_type=jnp.float32)
        return (context, logsum[:, 0])
    context, logsum = lax.map(per_head, (split_heads(queries), split_heads(key_rows), split_heads(value_rows)))
    return (merge_heads(context).astype(jnp.bfloat16), logsum)

def attend_back(queries, key_rows, value_rows, allowed, logsum, grad_context):

    def per_head(operands):
        query_head, key_head, value_head, logsum_head, grad_head = operands
        scaling = query_head.shape[-1] ** (-0.5)
        weights_full = jnp.exp(head_scores(query_head, key_head, allowed) - logsum_head[:, None])
        value_grad = jnp.dot(weights_full.astype(jnp.bfloat16).T, grad_head, preferred_element_type=jnp.float32)
        grad_prob = jnp.dot(grad_head, value_head.T, preferred_element_type=jnp.float32)
        row_total = lax.optimization_barrier(jnp.sum(weights_full * grad_prob, axis=-1, keepdims=True))
        grad_scores = (weights_full * (grad_prob - row_total) * scaling).astype(jnp.bfloat16)
        query_grad = jnp.dot(grad_scores, key_head, preferred_element_type=jnp.float32)
        key_grad = jnp.dot(grad_scores.T, query_head, preferred_element_type=jnp.float32)
        return (query_grad, key_grad, value_grad)
    query_grad, key_grad, value_grad = lax.map(per_head, (split_heads(queries), split_heads(key_rows), split_heads(value_rows), logsum, split_heads(grad_context)))
    return (merge_heads(query_grad), merge_heads(key_grad), merge_heads(value_grad))

def reference(inputs, lengths, cotangent, norm1_gain, norm1_bias, qkv_weight, query_bias, value_bias, out_weight, out_bias, norm2_gain, norm2_bias, up_weight, up_bias, down_weight, down_bias):
    gain_one = norm1_gain.astype(jnp.float32)
    shift_one = norm1_bias.astype(jnp.float32)
    gain_two = norm2_gain.astype(jnp.float32)
    shift_two = norm2_bias.astype(jnp.float32)
    positions = jnp.arange(L, dtype=jnp.int32)

    def one_sequence(carry, operands):
        tokens, length, grad_given = operands
        allowed = (positions[None, :] <= positions[:, None]) & (positions[None, :] < length)
        start = tokens.astype(jnp.float32)
        normed1, inv_std1, shifted1 = layer_norm(start, gain_one, shift_one)
        attn_in = shifted1.astype(jnp.bfloat16)
        projected = jnp.dot(attn_in, qkv_weight, preferred_element_type=jnp.float32)
        queries = (projected[:, :D] + query_bias.astype(jnp.float32)).astype(jnp.bfloat16)
        key_rows = projected[:, D:2 * D].astype(jnp.bfloat16)
        value_rows = (projected[:, 2 * D:] + value_bias.astype(jnp.float32)).astype(jnp.bfloat16)
        context, logsum = attend(queries, key_rows, value_rows, allowed)
        resid = start + jnp.dot(context, out_weight, preferred_element_type=jnp.float32) + out_bias.astype(jnp.float32)
        normed2, inv_std2, shifted2 = layer_norm(resid, gain_two, shift_two)
        mlp_in = shifted2.astype(jnp.bfloat16)
        pre_act = jnp.dot(mlp_in, up_weight, preferred_element_type=jnp.float32) + up_bias.astype(jnp.float32)
        act_value, act_slope = gelu_parts(pre_act)
        hidden = act_value.astype(jnp.bfloat16)
        result = (resid + jnp.dot(hidden, down_weight, preferred_element_type=jnp.float32) + down_bias.astype(jnp.float32)).astype(jnp.bfloat16)
        live_rows = (positions < length).astype(jnp.float32)[:, None]
        grad_out = grad_given.astype(jnp.float32) * live_rows
        grad_out_b = grad_out.astype(jnp.bfloat16)
        down_w_grad = jnp.dot(hidden.T, grad_out_b, preferred_element_type=jnp.float32)
        down_b_grad = lax.optimization_barrier(jnp.sum(grad_out, axis=0))
        grad_pre = jnp.dot(grad_out_b, down_weight.T, preferred_element_type=jnp.float32) * act_slope
        up_b_grad = lax.optimization_barrier(jnp.sum(grad_pre, axis=0))
        grad_pre_b = grad_pre.astype(jnp.bfloat16)
        up_w_grad = jnp.dot(mlp_in.T, grad_pre_b, preferred_element_type=jnp.float32)
        grad_mlp_in = jnp.dot(grad_pre_b, up_weight.T, preferred_element_type=jnp.float32)
        gain2_grad = lax.optimization_barrier(jnp.sum(grad_mlp_in * normed2, axis=0))
        shift2_grad = lax.optimization_barrier(jnp.sum(grad_mlp_in, axis=0))
        grad_resid = grad_out + norm_back(grad_mlp_in, normed2, inv_std2, gain_two)
        out_b_grad = lax.optimization_barrier(jnp.sum(grad_resid, axis=0))
        grad_resid_b = grad_resid.astype(jnp.bfloat16)
        out_w_grad = jnp.dot(context.T, grad_resid_b, preferred_element_type=jnp.float32)
        grad_context = jnp.dot(grad_resid_b, out_weight.T, preferred_element_type=jnp.float32).astype(jnp.bfloat16)
        query_grad, key_grad, value_grad = attend_back(queries, key_rows, value_rows, allowed, logsum, grad_context)
        query_b_grad = lax.optimization_barrier(jnp.sum(query_grad, axis=0))
        value_b_grad = lax.optimization_barrier(jnp.sum(value_grad, axis=0))
        grad_qkv = jnp.concatenate([query_grad, key_grad, value_grad], axis=1).astype(jnp.bfloat16)
        qkv_w_grad = jnp.dot(attn_in.T, grad_qkv, preferred_element_type=jnp.float32)
        grad_attn_in = jnp.dot(grad_qkv, qkv_weight.T, preferred_element_type=jnp.float32)
        gain1_grad = lax.optimization_barrier(jnp.sum(grad_attn_in * normed1, axis=0))
        shift1_grad = lax.optimization_barrier(jnp.sum(grad_attn_in, axis=0))
        grad_input = grad_resid + norm_back(grad_attn_in, normed1, inv_std1, gain_one)
        terms = (gain1_grad, shift1_grad, qkv_w_grad, query_b_grad, value_b_grad, out_w_grad, out_b_grad, gain2_grad, shift2_grad, up_w_grad, up_b_grad, down_w_grad, down_b_grad)
        carry = tuple((total + term for total, term in zip(carry, terms)))
        return (carry, (result, grad_input))
    zero_carry = (jnp.zeros((D,), jnp.float32), jnp.zeros((D,), jnp.float32), jnp.zeros((D, 3 * D), jnp.float32), jnp.zeros((D,), jnp.float32), jnp.zeros((D,), jnp.float32), jnp.zeros((D, D), jnp.float32), jnp.zeros((D,), jnp.float32), jnp.zeros((D,), jnp.float32), jnp.zeros((D,), jnp.float32), jnp.zeros((D, FF), jnp.float32), jnp.zeros((FF,), jnp.float32), jnp.zeros((FF, D), jnp.float32), jnp.zeros((D,), jnp.float32))
    totals, (outputs, input_grad) = lax.scan(one_sequence, zero_carry, (inputs, lengths.astype(jnp.int32), cotangent))
    return (outputs, input_grad, totals[0], totals[1], totals[2], totals[3], totals[4], totals[5], totals[6], totals[7], totals[8], totals[9], totals[10], totals[11], totals[12])
```

```python
import functools

import jax
import jax.numpy as jnp
from jax import lax
from jax.experimental import pallas as pl
from jax.experimental.pallas import tpu as pltpu
from jax.sharding import PartitionSpec as P

HD = 64
LANES = 128
EPS = 1e-05
GELU_C = 0.7978845608028654
MASKED = -1e30
BF = jnp.bfloat16
F32 = jnp.float32


def mm(a, b, dims=((1,), (0,))):
    return lax.dot_general(a, b, (dims, ((), ())), preferred_element_type=F32)


NT = ((1,), (1,))
TN = ((0,), (0,))


def ln_stats(x):
    average = jnp.mean(x, axis=-1, keepdims=True)
    centered = x - average
    variance = jnp.mean(centered * centered, axis=-1, keepdims=True)
    inv = lax.rsqrt(variance + EPS)
    return centered * inv, inv


def ln_back(grad_in, normed, inv, gain):
    scaled = grad_in * gain
    return inv * (
        scaled
        - jnp.mean(scaled, axis=-1, keepdims=True)
        - normed * jnp.mean(scaled * normed, axis=-1, keepdims=True)
    )


def gelu_parts(pre):
    tangent = jnp.tanh(GELU_C * (pre + 0.044715 * pre * pre * pre))
    result = 0.5 * pre * (1.0 + tangent)
    slope = 0.5 * (1.0 + tangent) + 0.5 * pre * (1.0 - tangent * tangent) * GELU_C * (
        1.0 + 3.0 * 0.044715 * pre * pre
    )
    return result, slope


def head_mask(rows, which):
    lane = lax.broadcasted_iota(jnp.int32, (rows, LANES), 1)
    return (lane >= HD) if which else (lane < HD)


def allowed_keys(meta, keys, rows):
    key = lax.broadcasted_iota(jnp.int32, (keys, rows), 0)
    row = lax.broadcasted_iota(jnp.int32, (keys, rows), 1) + meta[0]
    return (key <= row) & (key < meta[1])


def attend_kernel(meta, q_ref, kv_ref, ctx_ref, lse_ref):
    rows = q_ref.shape[0]
    keys = kv_ref.shape[0]
    k = kv_ref[:, :LANES]
    vt = kv_ref[:, LANES:].T
    q = q_ref[...] * jnp.asarray(HD ** -0.5, BF)
    allowed = allowed_keys(meta, keys, rows)
    pieces = []
    for which in range(2):
        qm = jnp.where(head_mask(rows, which), q, jnp.zeros_like(q))
        s = jnp.where(allowed, mm(k, qm, NT), MASKED)
        top = jnp.max(s, axis=0, keepdims=True)
        e = jnp.exp(s - top)
        total = jnp.sum(e, axis=0, keepdims=True)
        weights = (e * (1.0 / total)).astype(BF)
        pieces.append(mm(vt[which * HD:(which + 1) * HD], weights))
        lse_ref[0, which:which + 1, :] = top + jnp.log(total)
    ctx_ref[...] = jnp.concatenate(pieces, axis=0).T.astype(BF)


def attend(meta, q, kv):
    rows, width = q.shape
    keys = kv.shape[0]
    pairs = width // LANES
    return pl.pallas_call(
        attend_kernel,
        grid_spec=pltpu.PrefetchScalarGridSpec(
            num_scalar_prefetch=1,
            grid=(pairs,),
            in_specs=[
                pl.BlockSpec((rows, LANES), lambda p, m: (0, p)),
                pl.BlockSpec((keys, 2 * LANES), lambda p, m: (0, p)),
            ],
            out_specs=[
                pl.BlockSpec((rows, LANES), lambda p, m: (0, p)),
                pl.BlockSpec((1, 2, rows), lambda p, m: (p, 0, 0)),
            ],
        ),
        out_shape=[
            jax.ShapeDtypeStruct((rows, width), BF),
            jax.ShapeDtypeStruct((pairs, 2, rows), F32),
        ],
        name="attend",
    )(meta, q, kv)


def attend_back_kernel(meta, q_ref, kv_ref, lse_ref, g_ref, dq_ref, dkv_ref):
    rows = q_ref.shape[0]
    keys = kv_ref.shape[0]
    scale = jnp.asarray(HD ** -0.5, BF)
    k = kv_ref[:, :LANES]
    v = kv_ref[:, LANES:]
    kt = k.T
    q = q_ref[...]
    g = g_ref[...]
    allowed = allowed_keys(meta, keys, rows)
    dq, weights_all, ds_all, q_all, g_all = [], [], [], [], []
    for which in range(2):
        mask = head_mask(rows, which)
        qm = jnp.where(mask, q, jnp.zeros_like(q))
        gm = jnp.where(mask, g, jnp.zeros_like(g))
        s = jnp.where(allowed, mm(k, qm * scale, NT), MASKED)
        weights = jnp.exp(s - lse_ref[0, which:which + 1, :])
        dprob = mm(v, gm * scale, NT)
        delta = jnp.sum(weights * dprob, axis=0, keepdims=True)
        ds = (weights * (dprob - delta)).astype(BF)
        dq.append(mm(kt[which * HD:(which + 1) * HD], ds))
        weights_all.append(weights.astype(BF))
        ds_all.append(ds)
        q_all.append(qm)
        g_all.append(gm)
    dq_ref[...] = jnp.concatenate(dq, axis=0).T.astype(BF)
    dk = mm(jnp.concatenate(ds_all, axis=1), jnp.concatenate(q_all, axis=0))
    dv = mm(jnp.concatenate(weights_all, axis=1), jnp.concatenate(g_all, axis=0))
    dkv_ref[:, :LANES] = dk.astype(BF)
    dkv_ref[:, LANES:] = dv.astype(BF)


def attend_back(meta, q, kv, lse, g):
    rows, width = q.shape
    keys = kv.shape[0]
    pairs = width // LANES
    return pl.pallas_call(
        attend_back_kernel,
        grid_spec=pltpu.PrefetchScalarGridSpec(
            num_scalar_prefetch=1,
            grid=(pairs,),
            in_specs=[
                pl.BlockSpec((rows, LANES), lambda p, m: (0, p)),
                pl.BlockSpec((keys, 2 * LANES), lambda p, m: (0, p)),
                pl.BlockSpec((1, 2, rows), lambda p, m: (p, 0, 0)),
                pl.BlockSpec((rows, LANES), lambda p, m: (0, p)),
            ],
            out_specs=[
                pl.BlockSpec((rows, LANES), lambda p, m: (0, p)),
                pl.BlockSpec((keys, 2 * LANES), lambda p, m: (0, p)),
            ],
        ),
        out_shape=[
            jax.ShapeDtypeStruct((rows, width), BF),
            jax.ShapeDtypeStruct((keys, 2 * width), BF),
        ],
        name="attend_back",
    )(meta, q, kv, lse, g)


def swap(x, bit):
    n = lax.axis_size("dp")
    return lax.ppermute(x, "dp", [(i, i ^ bit) for i in range(n)])


def gather_dp(x):
    n = lax.axis_size("dp")
    if n != 8:
        return lax.all_gather(x, "dp", axis=0)
    me = lax.axis_index("dp")
    group, core = me // 2, me % 2
    half = jnp.zeros((n // 2,) + x.shape, x.dtype)
    half = lax.dynamic_update_slice(half, x[None], (group, 0, 0))
    for d in range(1, n // 2):
        got = swap(x, 2 * d)
        half = lax.dynamic_update_slice(half, got[None], (group ^ d, 0, 0))
    other = swap(half, 1)
    even = jnp.where(core == 0, half, other)
    odd = jnp.where(core == 0, other, half)
    return jnp.stack([even, odd], axis=1).reshape((n,) + x.shape)


def scatter_dp(g):
    n = lax.axis_size("dp")
    if n != 8:
        return lax.psum_scatter(g, "dp", scatter_dimension=0).astype(F32)
    me = lax.axis_index("dp")
    group, core = me // 2, me % 2
    pairs = g.reshape((n // 2, 2) + g.shape[1:])
    keep = lax.dynamic_index_in_dim(pairs, core, 1, keepdims=False)
    send = lax.dynamic_index_in_dim(pairs, 1 - core, 1, keepdims=False)
    got = swap(send, 1)
    summed = (keep.astype(F32) + got.astype(F32)).astype(BF)
    total = lax.dynamic_index_in_dim(summed, group, 0, keepdims=False).astype(F32)
    for d in range(1, n // 2):
        part = lax.dynamic_index_in_dim(summed, group ^ d, 0, keepdims=False)
        total = total + swap(part, 2 * d).astype(F32)
    return total


def gather_z(x):
    return lax.all_gather(x, "seq", axis=0, tiled=True)


def scatter_z(x):
    return lax.psum_scatter(x, "seq", scatter_dimension=0, tiled=True).astype(F32)


def pad_cols(x, width):
    return jnp.pad(x, [(0, 0)] * (x.ndim - 1) + [(0, width - x.shape[-1])])


def pair_up(a, b):
    lead = a.shape[:-1]
    blocks = a.shape[-1] // LANES
    both = jnp.stack([a.reshape(lead + (blocks, LANES)), b.reshape(lead + (blocks, LANES))], axis=-2)
    return both.reshape(lead + (2 * a.shape[-1],))


def pair_split(x):
    lead = x.shape[:-1]
    both = x.reshape(lead + (x.shape[-1] // (2 * LANES), 2, LANES))
    half = lead + (x.shape[-1] // 2,)
    return both[..., 0, :].reshape(half), both[..., 1, :].reshape(half)


def shards(
    inputs,
    lengths,
    cotangent,
    norm1_gain,
    norm1_bias,
    qkv_weight,
    query_bias,
    value_bias,
    out_weight,
    out_bias,
    norm2_gain,
    norm2_bias,
    up_weight,
    up_bias,
    down_weight,
    down_bias,
):
    n = lax.axis_size("dp")
    zs = lax.axis_size("seq")
    z = lax.axis_index("seq")
    rows, width = inputs.shape[1:]
    total_rows = rows * zs
    share = norm1_gain.shape[0]
    wide = -(-width // LANES) * LANES
    qkv_cols = qkv_weight.shape[1]
    ff = up_weight.shape[1]
    ff_total = ff * zs
    length = lengths[0]
    first = z * rows
    meta = jnp.stack([first, length]).astype(jnp.int32)

    thin = jnp.stack(
        [norm1_gain, norm1_bias, query_bias, value_bias, out_bias, norm2_gain, norm2_bias, down_bias]
    ).reshape(1, 8 * share)
    thin_all = lax.all_gather(
        jnp.concatenate([thin, up_bias.reshape(1, -1)], axis=1), "dp", axis=0
    ).reshape(n, 8 * share + up_bias.shape[0])
    vectors = (
        thin_all[:, : 8 * share].reshape(n, 8, share).transpose(1, 0, 2).reshape(8, width).astype(F32)
    )
    up_bias_all = thin_all[:, 8 * share:].reshape(ff_total).astype(F32)
    gain1, shift1, bias_q, bias_v, bias_o, gain2, shift2, bias_d = [vectors[i] for i in range(8)]
    up_shift = lax.dynamic_slice_in_dim(up_bias_all, z * ff, ff)

    attn_w = lax.all_gather(jnp.concatenate([qkv_weight, out_weight], axis=1), "seq", axis=0)
    x_full = gather_z(inputs[0])
    mlp_w = gather_dp(jnp.concatenate([up_weight, down_weight.T], axis=1)).reshape(width, 2 * ff)
    up_full = mlp_w[:, :ff]
    down_t = mlp_w[:, ff:]

    qkv_rows = attn_w[:, :, :qkv_cols].transpose(1, 0, 2).reshape(share, 3 * width)
    wq_s = pad_cols(qkv_rows[:, :width], wide)
    wk_s = pad_cols(qkv_rows[:, width : 2 * width], wide)
    wv_s = pad_cols(qkv_rows[:, 2 * width :], wide)
    qkv_full = gather_dp(jnp.concatenate([wq_s, pair_up(wk_s, wv_s)], axis=1)).reshape(width, 3 * wide)
    wq = qkv_full[:, :wide]
    wkv = qkv_full[:, wide:]
    out_rows = attn_w[:, :, qkv_cols:].transpose(1, 0, 2).reshape(share, width)
    wo = gather_dp(out_rows).reshape(width, width)
    g_full = gather_z(cotangent[0])

    x_own = inputs[0].astype(F32)
    normed1, inv1 = ln_stats(x_own)
    attn_own = (normed1 * gain1 + shift1).astype(BF)
    normed1_full, _ = ln_stats(x_full.astype(F32))
    attn_full = (normed1_full * gain1 + shift1).astype(BF)
    q = (mm(attn_own, wq) + pad_cols(bias_q, wide)).astype(BF)
    bias_kv = pair_up(jnp.zeros((wide,), F32), pad_cols(bias_v, wide))
    kv = (mm(attn_full, wkv) + bias_kv).astype(BF)
    ctx, lse = attend(meta, q, kv)
    ctx = ctx[:, :width]
    resid = x_own + mm(ctx, wo) + bias_o
    normed2, inv2 = ln_stats(resid)
    mlp_in = (normed2 * gain2 + shift2).astype(BF)
    mlp_full = gather_z(mlp_in)
    pre = mm(mlp_full, up_full) + up_shift
    act, slope = gelu_parts(pre)
    hidden = act.astype(BF)

    position = lax.broadcasted_iota(jnp.int32, (total_rows, 1), 0)
    g_full = g_full * (position < length).astype(BF)
    own_position = first + lax.broadcasted_iota(jnp.int32, (rows, 1), 0)
    grad_out = cotangent[0].astype(F32) * (own_position < length).astype(F32)
    grad_pre = mm(g_full, down_t) * slope
    grad_pre_b = grad_pre.astype(BF)
    grad_mlp = scatter_z(mm(grad_pre_b, up_full, NT).astype(BF))
    mlp_out = scatter_z(mm(hidden, down_t, NT).astype(BF))
    outputs = (resid + mlp_out + bias_d).astype(BF)
    up_b_block = jnp.sum(grad_pre, axis=0)
    mlp_dw = jnp.concatenate([mm(mlp_full, grad_pre_b, TN), mm(g_full, hidden, TN)], axis=1).astype(BF)
    mlp_dw = scatter_dp(mlp_dw.reshape(n, share, 2 * ff))
    up_grad = mlp_dw[:, :ff]
    down_grad = mlp_dw[:, ff:].T

    grad_resid = grad_out + ln_back(grad_mlp, normed2, inv2, gain2)
    grad_resid_b = grad_resid.astype(BF)
    grad_ctx = pad_cols(mm(grad_resid_b, wo, NT).astype(BF), wide)
    dq, dkv = attend_back(meta, q, kv, lse, grad_ctx)
    part = mm(dkv, wkv, NT)
    grad_attn = scatter_z(part.astype(BF)) + mm(dq, wq, NT)

    dwq = mm(attn_own, dq, TN)[:, :width]
    dwk, dwv = pair_split(mm(attn_full, dkv, TN))
    dwo = mm(ctx, grad_resid_b, TN)
    attn_dw = jnp.concatenate(
        [
            jnp.concatenate([dwq, dwk[:, :width], dwv[:, :width]], axis=1)
            .astype(BF)
            .reshape(n, share, zs, qkv_cols)
            .transpose(2, 0, 1, 3),
            dwo.astype(BF).reshape(n, share, zs, width // zs).transpose(2, 0, 1, 3),
        ],
        axis=3,
    )
    piece = qkv_cols + width // zs
    attn_dw = scatter_dp(attn_dw.transpose(1, 0, 2, 3).reshape(n, zs * share, piece))
    attn_dw = scatter_z(attn_dw.astype(BF)).reshape(share, piece)

    dv = pair_split(dkv)[1][:, :width]
    input_grad = grad_resid + ln_back(grad_attn, normed1, inv1, gain1)
    vec = jnp.stack(
        [
            jnp.sum(grad_attn * normed1, axis=0),
            jnp.sum(grad_attn, axis=0),
            jnp.sum(dq.astype(F32), axis=0)[:width],
            jnp.sum(dv.astype(F32), axis=0),
            jnp.sum(grad_resid, axis=0),
            jnp.sum(grad_mlp * normed2, axis=0),
            jnp.sum(grad_mlp, axis=0),
            jnp.sum(grad_out, axis=0),
        ]
    )
    up_b = lax.dynamic_update_slice_in_dim(jnp.zeros((ff_total,), F32), up_b_block, z * ff, 0)
    thin_grad = jnp.concatenate(
        [vec.reshape(8, n, share).transpose(1, 0, 2).reshape(n, 8 * share), up_b.reshape(n, ff_total // n)],
        axis=1,
    )
    thin_grad = lax.psum(lax.psum_scatter(thin_grad, "dp", scatter_dimension=0), "seq")
    vec_out = thin_grad[: 8 * share].reshape(8, share)
    return (
        outputs[None],
        input_grad[None],
        vec_out[0],
        vec_out[1],
        attn_dw[:, :qkv_cols],
        vec_out[2],
        vec_out[3],
        attn_dw[:, qkv_cols:],
        vec_out[4],
        vec_out[5],
        vec_out[6],
        up_grad,
        thin_grad[8 * share:],
        down_grad,
        vec_out[7],
    )


def solution(mesh):
    row = P("dp", "seq", None)
    vec = P("dp")
    mat = P("dp", "seq")
    in_specs = (row, vec, row, vec, vec, mat, vec, vec, mat, vec, vec, vec, mat, vec, P("seq", "dp"), vec)
    out_specs = (row, row, vec, vec, mat, vec, vec, mat, vec, vec, vec, mat, vec, P("seq", "dp"), vec)
    return jax.shard_map(shards, mesh=mesh, in_specs=in_specs, out_specs=out_specs, check_vma=False)
```

```python
import functools

import jax
import jax.numpy as jnp
from jax import lax
from jax.experimental import pallas as pl
from jax.experimental.pallas import tpu as pltpu
from jax.sharding import PartitionSpec as P

HD = 64
LANES = 128
EPS = 1e-05
GELU_C = 0.7978845608028654
MASKED = -1e30
BF = jnp.bfloat16
F32 = jnp.float32


def mm(a, b, dims=((1,), (0,))):
    return lax.dot_general(a, b, (dims, ((), ())), preferred_element_type=F32)


NT = ((1,), (1,))
TN = ((0,), (0,))


def ln_stats(x):
    average = jnp.mean(x, axis=-1, keepdims=True)
    centered = x - average
    variance = jnp.mean(centered * centered, axis=-1, keepdims=True)
    inv = lax.rsqrt(variance + EPS)
    return centered * inv, inv


def ln_back(grad_in, normed, inv, gain):
    scaled = grad_in * gain
    return inv * (
        scaled
        - jnp.mean(scaled, axis=-1, keepdims=True)
        - normed * jnp.mean(scaled * normed, axis=-1, keepdims=True)
    )


def gelu_parts(pre):
    tangent = jnp.tanh(GELU_C * (pre + 0.044715 * pre * pre * pre))
    result = 0.5 * pre * (1.0 + tangent)
    slope = 0.5 * (1.0 + tangent) + 0.5 * pre * (1.0 - tangent * tangent) * GELU_C * (
        1.0 + 3.0 * 0.044715 * pre * pre
    )
    return result, slope


def head_mask(rows, which):
    lane = lax.broadcasted_iota(jnp.int32, (rows, LANES), 1)
    return (lane >= HD) if which else (lane < HD)


def allowed_keys(meta, keys, rows):
    key = lax.broadcasted_iota(jnp.int32, (keys, rows), 0)
    row = lax.broadcasted_iota(jnp.int32, (keys, rows), 1) + meta[0]
    return (key <= row) & (key < meta[1])


def attend_kernel(meta, q_ref, kv_ref, ctx_ref, lse_ref):
    rows = q_ref.shape[0]
    keys = kv_ref.shape[0]
    k = kv_ref[:, :LANES]
    vt = kv_ref[:, LANES:].T
    q = q_ref[...] * jnp.asarray(HD ** -0.5, BF)
    allowed = allowed_keys(meta, keys, rows)
    pieces = []
    for which in range(2):
        qm = jnp.where(head_mask(rows, which), q, jnp.zeros_like(q))
        s = jnp.where(allowed, mm(k, qm, NT), MASKED)
        top = jnp.max(s, axis=0, keepdims=True)
        e = jnp.exp(s - top)
        total = jnp.sum(e, axis=0, keepdims=True)
        weights = (e * (1.0 / total)).astype(BF)
        pieces.append(mm(vt[which * HD:(which + 1) * HD], weights))
        lse_ref[0, which:which + 1, :] = top + jnp.log(total)
    ctx_ref[...] = jnp.concatenate(pieces, axis=0).T.astype(BF)


def attend(meta, q, kv):
    rows, width = q.shape
    keys = kv.shape[0]
    pairs = width // LANES
    return pl.pallas_call(
        attend_kernel,
        grid_spec=pltpu.PrefetchScalarGridSpec(
            num_scalar_prefetch=1,
            grid=(pairs,),
            in_specs=[
                pl.BlockSpec((rows, LANES), lambda p, m: (0, p)),
                pl.BlockSpec((keys, 2 * LANES), lambda p, m: (0, p)),
            ],
            out_specs=[
                pl.BlockSpec((rows, LANES), lambda p, m: (0, p)),
                pl.BlockSpec((1, 2, rows), lambda p, m: (p, 0, 0)),
            ],
        ),
        out_shape=[
            jax.ShapeDtypeStruct((rows, width), BF),
            jax.ShapeDtypeStruct((pairs, 2, rows), F32),
        ],
        cost_estimate=pl.CostEstimate(
            flops=8 * rows * keys * width, transcendentals=2 * pairs * rows * keys, bytes_accessed=6 * keys * width
        ),
        name="attend",
    )(meta, q, kv)


def attend_back_kernel(meta, q_ref, kv_ref, lse_ref, g_ref, dq_ref, dkv_ref):
    rows = q_ref.shape[0]
    keys = kv_ref.shape[0]
    scale = jnp.asarray(HD ** -0.5, BF)
    k = kv_ref[:, :LANES]
    v = kv_ref[:, LANES:]
    kt = k.T
    q = q_ref[...]
    g = g_ref[...]
    allowed = allowed_keys(meta, keys, rows)
    dq, weights_all, ds_all, q_all, g_all = [], [], [], [], []
    for which in range(2):
        mask = head_mask(rows, which)
        qm = jnp.where(mask, q, jnp.zeros_like(q))
        gm = jnp.where(mask, g, jnp.zeros_like(g))
        s = jnp.where(allowed, mm(k, qm * scale, NT), MASKED)
        weights = jnp.exp(s - lse_ref[0, which:which + 1, :])
        dprob = mm(v, gm * scale, NT)
        delta = jnp.sum(weights * dprob, axis=0, keepdims=True)
        ds = (weights * (dprob - delta)).astype(BF)
        dq.append(mm(kt[which * HD:(which + 1) * HD], ds))
        weights_all.append(weights.astype(BF))
        ds_all.append(ds)
        q_all.append(qm)
        g_all.append(gm)
    dq_ref[...] = jnp.concatenate(dq, axis=0).T.astype(BF)
    dk = mm(jnp.concatenate(ds_all, axis=1), jnp.concatenate(q_all, axis=0))
    dv = mm(jnp.concatenate(weights_all, axis=1), jnp.concatenate(g_all, axis=0))
    dkv_ref[:, :LANES] = dk.astype(BF)
    dkv_ref[:, LANES:] = dv.astype(BF)


def attend_back(meta, q, kv, lse, g):
    rows, width = q.shape
    keys = kv.shape[0]
    pairs = width // LANES
    return pl.pallas_call(
        attend_back_kernel,
        grid_spec=pltpu.PrefetchScalarGridSpec(
            num_scalar_prefetch=1,
            grid=(pairs,),
            in_specs=[
                pl.BlockSpec((rows, LANES), lambda p, m: (0, p)),
                pl.BlockSpec((keys, 2 * LANES), lambda p, m: (0, p)),
                pl.BlockSpec((1, 2, rows), lambda p, m: (p, 0, 0)),
                pl.BlockSpec((rows, LANES), lambda p, m: (0, p)),
            ],
            out_specs=[
                pl.BlockSpec((rows, LANES), lambda p, m: (0, p)),
                pl.BlockSpec((keys, 2 * LANES), lambda p, m: (0, p)),
            ],
        ),
        out_shape=[
            jax.ShapeDtypeStruct((rows, width), BF),
            jax.ShapeDtypeStruct((keys, 2 * width), BF),
        ],
        cost_estimate=pl.CostEstimate(
            flops=20 * rows * keys * width, transcendentals=2 * pairs * rows * keys, bytes_accessed=12 * keys * width
        ),
        name="attend_back",
    )(meta, q, kv, lse, g)


def swap(x, bit):
    n = lax.axis_size("dp")
    return lax.ppermute(x, "dp", [(i, i ^ bit) for i in range(n)])


def gather_dp(x, after=None):
    n = lax.axis_size("dp")
    if n != 8:
        return lax.all_gather(x, "dp", axis=0)
    me = lax.axis_index("dp")
    group, core = me // 2, me % 2
    half = jnp.zeros((n // 2,) + x.shape, x.dtype)
    half = lax.dynamic_update_slice(half, x[None], (group, 0, 0))
    for d in range(1, n // 2):
        got = swap(x, 2 * d)
        if after is not None:
            got, after = lax.optimization_barrier((got, after))
        half = lax.dynamic_update_slice(half, got[None], (group ^ d, 0, 0))
    other = swap(half, 1)
    full = jnp.zeros((n // 2, 2) + x.shape, x.dtype)
    full = lax.dynamic_update_slice(full, half[:, None], (0, core, 0, 0))
    full = lax.dynamic_update_slice(full, other[:, None], (0, 1 - core, 0, 0))
    return full.reshape((n,) + x.shape)


def scatter_dp(g):
    n = lax.axis_size("dp")
    if n != 8:
        return lax.psum_scatter(g, "dp", scatter_dimension=0).astype(F32)
    me = lax.axis_index("dp")
    group, core = me // 2, me % 2
    pairs = g.reshape((n // 2, 2) + g.shape[1:])
    keep = lax.dynamic_index_in_dim(pairs, core, 1, keepdims=False)
    send = lax.dynamic_index_in_dim(pairs, 1 - core, 1, keepdims=False)
    got = swap(send, 1)
    summed = (keep.astype(F32) + got.astype(F32)).astype(BF)
    total = lax.dynamic_index_in_dim(summed, group, 0, keepdims=False).astype(F32)
    for d in range(1, n // 2):
        part = lax.dynamic_index_in_dim(summed, group ^ d, 0, keepdims=False)
        total = total + swap(part, 2 * d).astype(F32)
    return total


def gather_z(x):
    return lax.all_gather(x, "seq", axis=0, tiled=True)


def scatter_z(x):
    return lax.psum_scatter(x, "seq", scatter_dimension=0, tiled=True).astype(F32)


def pad_cols(x, width):
    return jnp.pad(x, [(0, 0)] * (x.ndim - 1) + [(0, width - x.shape[-1])])


def pair_up(a, b):
    lead = a.shape[:-1]
    blocks = a.shape[-1] // LANES
    both = jnp.stack([a.reshape(lead + (blocks, LANES)), b.reshape(lead + (blocks, LANES))], axis=-2)
    return both.reshape(lead + (2 * a.shape[-1],))


def pair_split(x):
    lead = x.shape[:-1]
    both = x.reshape(lead + (x.shape[-1] // (2 * LANES), 2, LANES))
    half = lead + (x.shape[-1] // 2,)
    return both[..., 0, :].reshape(half), both[..., 1, :].reshape(half)


def shards(
    inputs,
    lengths,
    cotangent,
    norm1_gain,
    norm1_bias,
    qkv_weight,
    query_bias,
    value_bias,
    out_weight,
    out_bias,
    norm2_gain,
    norm2_bias,
    up_weight,
    up_bias,
    down_weight,
    down_bias,
):
    n = lax.axis_size("dp")
    zs = lax.axis_size("seq")
    z = lax.axis_index("seq")
    rows, width = inputs.shape[1:]
    total_rows = rows * zs
    share = norm1_gain.shape[0]
    wide = -(-width // LANES) * LANES
    qkv_cols = qkv_weight.shape[1]
    ff = up_weight.shape[1]
    ff_total = ff * zs
    length = lengths[0]
    first = z * rows
    meta = jnp.stack([first, length]).astype(jnp.int32)

    thin = jnp.stack(
        [norm1_gain, norm1_bias, query_bias, value_bias, out_bias, norm2_gain, norm2_bias, down_bias]
    ).reshape(1, 8 * share)
    thin_all = gather_dp(jnp.concatenate([thin, up_bias.reshape(1, -1)], axis=1))
    thin_all = thin_all.reshape(n, 8 * share + up_bias.shape[0])
    attn_w = lax.all_gather(jnp.concatenate([qkv_weight, out_weight], axis=1), "seq", axis=0)
    x_full = gather_z(inputs[0])
    mlp_w = gather_dp(jnp.concatenate([up_weight, down_weight.T], axis=1)).reshape(width, 2 * ff)
    attn_w, mlp_w, thin_all = lax.optimization_barrier((attn_w, mlp_w, thin_all))
    vectors = (
        thin_all[:, : 8 * share].reshape(n, 8, share).transpose(1, 0, 2).reshape(8, width).astype(F32)
    )
    up_bias_all = thin_all[:, 8 * share:].reshape(ff_total).astype(F32)
    gain1, shift1, bias_q, bias_v, bias_o, gain2, shift2, bias_d = [vectors[i] for i in range(8)]
    up_shift = lax.dynamic_slice_in_dim(up_bias_all, z * ff, ff)
    up_full = mlp_w[:, :ff]
    down_t = mlp_w[:, ff:]

    qkv_rows = attn_w[:, :, :qkv_cols].transpose(1, 0, 2).reshape(share, 3 * width)
    wq_s = pad_cols(qkv_rows[:, :width], wide)
    wk_s = pad_cols(qkv_rows[:, width : 2 * width], wide)
    wv_s = pad_cols(qkv_rows[:, 2 * width :], wide)
    qkv_full = gather_dp(jnp.concatenate([wq_s, pair_up(wk_s, wv_s)], axis=1)).reshape(width, 3 * wide)
    wq = qkv_full[:, :wide]
    wkv = qkv_full[:, wide:]
    out_rows = attn_w[:, :, qkv_cols:].transpose(1, 0, 2).reshape(share, width)
    out_rows, _ = lax.optimization_barrier((out_rows, qkv_full))
    cot, _ = lax.optimization_barrier((cotangent[0], x_full))
    g_full = gather_z(cot)

    x_own = inputs[0].astype(F32)
    normed1, inv1 = ln_stats(x_own)
    attn_own = (normed1 * gain1 + shift1).astype(BF)
    normed1_full, _ = ln_stats(x_full.astype(F32))
    attn_full = (normed1_full * gain1 + shift1).astype(BF)
    q = (mm(attn_own, wq) + pad_cols(bias_q, wide)).astype(BF)
    bias_kv = pair_up(jnp.zeros((wide,), F32), pad_cols(bias_v, wide))
    kv = (mm(attn_full, wkv) + bias_kv).astype(BF)
    wo = gather_dp(out_rows, kv).reshape(width, width)
    ctx, lse = attend(meta, q, kv)
    ctx, g_full = lax.optimization_barrier((ctx, g_full))
    ctx = ctx[:, :width]
    resid = x_own + mm(ctx, wo) + bias_o
    normed2, inv2 = ln_stats(resid)
    mlp_in = (normed2 * gain2 + shift2).astype(BF)
    mlp_full = gather_z(mlp_in)
    pre = mm(mlp_full, up_full) + up_shift
    act, slope = gelu_parts(pre)
    hidden = act.astype(BF)

    position = lax.broadcasted_iota(jnp.int32, (total_rows, 1), 0)
    g_full = g_full * (position < length).astype(BF)
    own_position = first + lax.broadcasted_iota(jnp.int32, (rows, 1), 0)
    grad_out = cotangent[0].astype(F32) * (own_position < length).astype(F32)
    grad_pre = mm(g_full, down_t) * slope
    grad_pre_b = grad_pre.astype(BF)
    grad_mlp = scatter_z(mm(grad_pre_b, up_full, NT).astype(BF))
    mlp_part, _ = lax.optimization_barrier((mm(hidden, down_t, NT).astype(BF), grad_mlp))
    mlp_out = scatter_z(mlp_part)
    up_b_block = jnp.sum(grad_pre, axis=0)
    mlp_dw = jnp.concatenate([mm(mlp_full, grad_pre_b, TN), mm(g_full, hidden, TN)], axis=1).astype(BF)
    mlp_dw = scatter_dp(mlp_dw.reshape(n, share, 2 * ff))

    grad_resid = grad_out + ln_back(grad_mlp, normed2, inv2, gain2)
    grad_resid_b = grad_resid.astype(BF)
    grad_ctx = pad_cols(mm(grad_resid_b, wo, NT).astype(BF), wide)
    dwo = scatter_dp(mm(ctx, grad_resid_b, TN).astype(BF).reshape(n, share, width))
    dq, dkv = attend_back(meta, q, kv, lse, grad_ctx)
    dq, dkv, mlp_dw, mlp_out = lax.optimization_barrier((dq, dkv, mlp_dw, mlp_out))
    outputs = (resid + mlp_out + bias_d).astype(BF)
    up_grad = mlp_dw[:, :ff]
    down_grad = mlp_dw[:, ff:].T
    part_kv = mm(dkv, wkv, NT)
    part_q = mm(dq, wq, NT)
    grad_attn = scatter_z(part_kv.astype(BF)) + part_q
    dw = jnp.concatenate([mm(attn_own, dq, TN), mm(attn_full, dkv, TN)], axis=1).astype(BF)
    dw = scatter_dp(dw.reshape(n, share, 3 * wide))
    input_grad = grad_resid + ln_back(grad_attn, normed1, inv1, gain1)

    dv_sum = pair_split(jnp.sum(dkv.astype(F32), axis=0))[1][:width]
    vec = jnp.stack(
        [
            jnp.sum(part_kv * normed1_full, axis=0) + jnp.sum(part_q * normed1, axis=0),
            jnp.sum(part_kv, axis=0) + jnp.sum(part_q, axis=0),
            jnp.sum(dq.astype(F32), axis=0)[:width],
            dv_sum,
            jnp.sum(grad_resid, axis=0),
            jnp.sum(grad_mlp * normed2, axis=0),
            jnp.sum(grad_mlp, axis=0),
            jnp.sum(grad_out, axis=0),
        ]
    )
    up_b = lax.dynamic_update_slice_in_dim(jnp.zeros((ff_total,), F32), up_b_block, z * ff, 0)
    thin_grad = jnp.concatenate(
        [vec.reshape(8, n, share).transpose(1, 0, 2).reshape(n, 8 * share), up_b.reshape(n, ff_total // n)],
        axis=1,
    )
    thin_len = thin_grad.shape[1]
    thin_grad = scatter_dp(thin_grad.astype(BF)[:, None, :])

    piece = qkv_cols + width // zs
    dwk, dwv = pair_split(dw[:, wide:])
    dw_cols = jnp.concatenate([dw[:, :width], dwk[:, :width], dwv[:, :width]], axis=1).astype(BF)
    dwo = dwo.astype(BF)
    extra = -(-thin_len // piece)
    thin_rows = pad_cols(thin_grad.astype(BF), extra * piece).reshape(extra, piece)
    lines = -(-(share + extra) // 16) * 16
    thin_rows = jnp.pad(thin_rows, [(0, lines - share - extra), (0, 0)])
    blocks = []
    for j in range(zs):
        blocks.append(
            jnp.concatenate(
                [
                    dw_cols[:, j * qkv_cols : (j + 1) * qkv_cols],
                    dwo[:, j * (width // zs) : (j + 1) * (width // zs)],
                ],
                axis=1,
            )
        )
        blocks.append(thin_rows)
    last = scatter_z(jnp.concatenate(blocks, axis=0))
    attn_dw = last[:share]
    thin_grad = last[share : share + extra].reshape(extra * piece)[:thin_len]
    vec_out = thin_grad[: 8 * share].reshape(8, share)
    return (
        outputs[None],
        input_grad[None],
        vec_out[0],
        vec_out[1],
        attn_dw[:, :qkv_cols],
        vec_out[2],
        vec_out[3],
        attn_dw[:, qkv_cols:],
        vec_out[4],
        vec_out[5],
        vec_out[6],
        up_grad,
        thin_grad[8 * share:],
        down_grad,
        vec_out[7],
    )


def solution(mesh):
    row = P("dp", "seq", None)
    vec = P("dp")
    mat = P("dp", "seq")
    in_specs = (row, vec, row, vec, vec, mat, vec, vec, mat, vec, vec, vec, mat, vec, P("seq", "dp"), vec)
    out_specs = (row, row, vec, vec, mat, vec, vec, mat, vec, vec, vec, mat, vec, P("seq", "dp"), vec)
    return jax.shard_map(shards, mesh=mesh, in_specs=in_specs, out_specs=out_specs, check_vma=False)
```

```python
import jax
import jax.numpy as jnp
from jax import lax
from jax.experimental import pallas as pl
from jax.experimental.pallas import tpu as pltpu
from jax.sharding import PartitionSpec as P


HD = 64
LANES = 128
EPS = 1e-05
GELU_C = 0.7978845608028654
MASKED = -1e30
BF = jnp.bfloat16
F32 = jnp.float32


def mm(a, b, dims=((1,), (0,))):
    return lax.dot_general(a, b, (dims, ((), ())), preferred_element_type=F32)


NT = ((1,), (1,))
TN = ((0,), (0,))


def ln_stats(x):
    average = jnp.mean(x, axis=-1, keepdims=True)
    centered = x - average
    variance = jnp.mean(centered * centered, axis=-1, keepdims=True)
    inv = lax.rsqrt(variance + EPS)
    return centered * inv, inv


def ln_back(grad_in, normed, inv, gain):
    scaled = grad_in * gain
    return inv * (
        scaled
        - jnp.mean(scaled, axis=-1, keepdims=True)
        - normed * jnp.mean(scaled * normed, axis=-1, keepdims=True)
    )


def gelu_parts(pre):
    tangent = jnp.tanh(GELU_C * (pre + 0.044715 * pre * pre * pre))
    result = 0.5 * pre * (1.0 + tangent)
    slope = 0.5 * (1.0 + tangent) + 0.5 * pre * (1.0 - tangent * tangent) * GELU_C * (
        1.0 + 3.0 * 0.044715 * pre * pre
    )
    return result, slope


def head_mask(rows, which):
    lane = lax.broadcasted_iota(jnp.int32, (rows, LANES), 1)
    return (lane >= HD) if which else (lane < HD)


def fill_mask(meta, mask_ref):
    key = lax.broadcasted_iota(jnp.int32, mask_ref.shape, 0)
    row = lax.broadcasted_iota(jnp.int32, mask_ref.shape, 1) + meta[0]
    mask_ref[...] = jnp.where((key <= row) & (key < meta[1]), 0.0, MASKED)


def attend_kernel(meta, q_ref, kv_ref, ctx_ref, lse_ref, mask_ref):
    rows = q_ref.shape[0]

    @pl.when(pl.program_id(0) == 0)
    def _():
        fill_mask(meta, mask_ref)

    k = kv_ref[:, :LANES]
    vt = kv_ref[:, LANES:].T
    q = q_ref[...] * jnp.asarray(HD ** -0.5, BF)
    pieces = []
    for which in range(2):
        qm = jnp.where(head_mask(rows, which), q, jnp.zeros_like(q))
        s = mm(k, qm, NT) + mask_ref[...]
        top = jnp.max(s, axis=0, keepdims=True)
        e = jnp.exp(s - top)
        total = jnp.sum(e, axis=0, keepdims=True)
        weights = (e * (1.0 / total)).astype(BF)
        pieces.append(mm(vt[which * HD:(which + 1) * HD], weights))
        lse_ref[0, which:which + 1, :] = top + jnp.log(total)
    ctx_ref[...] = jnp.concatenate(pieces, axis=0).T.astype(BF)


def attend(meta, q, kv):
    rows, width = q.shape
    keys = kv.shape[0]
    pairs = width // LANES
    return pl.pallas_call(
        attend_kernel,
        grid_spec=pltpu.PrefetchScalarGridSpec(
            num_scalar_prefetch=1,
            grid=(pairs,),
            in_specs=[
                pl.BlockSpec((rows, LANES), lambda p, m: (0, p)),
                pl.BlockSpec((keys, 2 * LANES), lambda p, m: (0, p)),
            ],
            out_specs=[
                pl.BlockSpec((rows, LANES), lambda p, m: (0, p)),
                pl.BlockSpec((1, 2, rows), lambda p, m: (p, 0, 0)),
            ],
            scratch_shapes=[pltpu.VMEM((keys, rows), F32)],
        ),
        out_shape=[
            jax.ShapeDtypeStruct((rows, width), BF),
            jax.ShapeDtypeStruct((pairs, 2, rows), F32),
        ],
        cost_estimate=pl.CostEstimate(
            flops=8 * rows * keys * width, transcendentals=2 * pairs * rows * keys, bytes_accessed=6 * keys * width
        ),
        name="attend",
    )(meta, q, kv)


def attend_back_kernel(meta, q_ref, kv_ref, lse_ref, g_ref, dq_ref, dkv_ref, mask_ref):
    rows = q_ref.shape[0]

    @pl.when(pl.program_id(0) == 0)
    def _():
        fill_mask(meta, mask_ref)

    scale = jnp.asarray(HD ** -0.5, BF)
    k = kv_ref[:, :LANES]
    v = kv_ref[:, LANES:]
    kt = k.T
    q = q_ref[...]
    g = g_ref[...]
    dq, weights_all, ds_all, q_all, g_all = [], [], [], [], []
    for which in range(2):
        mask = head_mask(rows, which)
        qm = jnp.where(mask, q, jnp.zeros_like(q))
        gm = jnp.where(mask, g, jnp.zeros_like(g))
        s = mm(k, qm * scale, NT) + mask_ref[...]
        weights = jnp.exp(s - lse_ref[0, which:which + 1, :])
        dprob = mm(v, gm * scale, NT)
        delta = jnp.sum(weights * dprob, axis=0, keepdims=True)
        ds = (weights * (dprob - delta)).astype(BF)
        dq.append(mm(kt[which * HD:(which + 1) * HD], ds))
        weights_all.append(weights.astype(BF))
        ds_all.append(ds)
        q_all.append(qm)
        g_all.append(gm)
    dq_ref[...] = jnp.concatenate(dq, axis=0).T.astype(BF)
    dk = mm(jnp.concatenate(ds_all, axis=1), jnp.concatenate(q_all, axis=0))
    dv = mm(jnp.concatenate(weights_all, axis=1), jnp.concatenate(g_all, axis=0))
    dkv_ref[:, :LANES] = dk.astype(BF)
    dkv_ref[:, LANES:] = dv.astype(BF)


def attend_back(meta, q, kv, lse, g):
    rows, width = q.shape
    keys = kv.shape[0]
    pairs = width // LANES
    return pl.pallas_call(
        attend_back_kernel,
        grid_spec=pltpu.PrefetchScalarGridSpec(
            num_scalar_prefetch=1,
            grid=(pairs,),
            in_specs=[
                pl.BlockSpec((rows, LANES), lambda p, m: (0, p)),
                pl.BlockSpec((keys, 2 * LANES), lambda p, m: (0, p)),
                pl.BlockSpec((1, 2, rows), lambda p, m: (p, 0, 0)),
                pl.BlockSpec((rows, LANES), lambda p, m: (0, p)),
            ],
            out_specs=[
                pl.BlockSpec((rows, LANES), lambda p, m: (0, p)),
                pl.BlockSpec((keys, 2 * LANES), lambda p, m: (0, p)),
            ],
            scratch_shapes=[pltpu.VMEM((keys, rows), F32)],
        ),
        out_shape=[
            jax.ShapeDtypeStruct((rows, width), BF),
            jax.ShapeDtypeStruct((keys, 2 * width), BF),
        ],
        cost_estimate=pl.CostEstimate(
            flops=20 * rows * keys * width, transcendentals=2 * pairs * rows * keys, bytes_accessed=12 * keys * width
        ),
        name="attend_back",
    )(meta, q, kv, lse, g)


def swap(x, bit):
    n = lax.axis_size("dp")
    return lax.ppermute(x, "dp", [(i, i ^ bit) for i in range(n)])


def ring_z(x):
    size = lax.axis_size("seq")
    me = lax.axis_index("seq")
    full = jnp.zeros((size,) + x.shape, x.dtype)
    full = lax.dynamic_update_slice(full, x[None], (me, 0, 0))
    for d in range(1, size):
        got = lax.ppermute(x, "seq", [(i, (i + d) % size) for i in range(size)])
        full = lax.dynamic_update_slice(full, got[None], ((me - d) % size, 0, 0))
    return full


def gather_dp(chunks):
    n = lax.axis_size("dp")
    if n != 8:
        return lax.all_gather(jnp.concatenate(chunks, axis=0), "dp", axis=0)
    me = lax.axis_index("dp")
    group, core = me // 2, me % 2
    rows = sum(x.shape[0] for x in chunks)
    full = jnp.zeros((n // 2, 2, rows, chunks[0].shape[1]), chunks[0].dtype)
    at = 0
    for x in chunks:
        half = jnp.zeros((n // 2,) + x.shape, x.dtype)
        half = lax.dynamic_update_slice(half, x[None], (group, 0, 0))
        for d in range(1, n // 2):
            got = swap(x, 2 * d)
            half = lax.dynamic_update_slice(half, got[None], (group ^ d, 0, 0))
        other = swap(half, 1)
        full = lax.dynamic_update_slice(full, half[:, None], (0, core, at, 0))
        full = lax.dynamic_update_slice(full, other[:, None], (0, 1 - core, at, 0))
        at += x.shape[0]
    return full.reshape(n, rows, chunks[0].shape[1])


def scatter_dp(g):
    n = lax.axis_size("dp")
    if n != 8:
        return lax.psum_scatter(g, "dp", scatter_dimension=0).astype(F32)
    me = lax.axis_index("dp")
    group, core = me // 2, me % 2
    pairs = g.reshape((n // 2, 2) + g.shape[1:])
    keep = lax.dynamic_index_in_dim(pairs, core, 1, keepdims=False)
    send = lax.dynamic_index_in_dim(pairs, 1 - core, 1, keepdims=False)
    got = swap(send, 1)
    summed = (keep.astype(F32) + got.astype(F32)).astype(BF)
    total = lax.dynamic_index_in_dim(summed, group, 0, keepdims=False).astype(F32)
    for d in range(1, n // 2):
        part = lax.dynamic_index_in_dim(summed, group ^ d, 0, keepdims=False)
        total = total + swap(part, 2 * d).astype(F32)
    return total


def gather_z(x):
    return lax.all_gather(x, "seq", axis=0, tiled=True)


def scatter_z(x):
    return lax.psum_scatter(x, "seq", scatter_dimension=0, tiled=True).astype(F32)


def pad_cols(x, width):
    return jnp.pad(x, [(0, 0)] * (x.ndim - 1) + [(0, width - x.shape[-1])])


def pair_up(a, b):
    lead = a.shape[:-1]
    blocks = a.shape[-1] // LANES
    both = jnp.stack([a.reshape(lead + (blocks, LANES)), b.reshape(lead + (blocks, LANES))], axis=-2)
    return both.reshape(lead + (2 * a.shape[-1],))


def pair_split(x):
    lead = x.shape[:-1]
    both = x.reshape(lead + (x.shape[-1] // (2 * LANES), 2, LANES))
    half = lead + (x.shape[-1] // 2,)
    return both[..., 0, :].reshape(half), both[..., 1, :].reshape(half)


def shards(
    inputs,
    lengths,
    cotangent,
    norm1_gain,
    norm1_bias,
    qkv_weight,
    query_bias,
    value_bias,
    out_weight,
    out_bias,
    norm2_gain,
    norm2_bias,
    up_weight,
    up_bias,
    down_weight,
    down_bias,
):
    n = lax.axis_size("dp")
    zs = lax.axis_size("seq")
    z = lax.axis_index("seq")
    rows, width = inputs.shape[1:]
    total_rows = rows * zs
    share = norm1_gain.shape[0]
    wide = -(-width // LANES) * LANES
    qkv_cols = qkv_weight.shape[1]
    ff = up_weight.shape[1]
    ff_total = ff * zs
    length = lengths[0]
    first = z * rows
    meta = jnp.stack([first, length]).astype(jnp.int32)

    thin = jnp.stack(
        [norm1_gain, norm1_bias, query_bias, value_bias, out_bias, norm2_gain, norm2_bias, down_bias]
    ).reshape(1, 8 * share)
    thin_all = gather_dp([jnp.concatenate([thin, up_bias.reshape(1, -1)], axis=1)])
    thin_all = thin_all.reshape(n, 8 * share + up_bias.shape[0])
    vectors = (
        thin_all[:, : 8 * share].reshape(n, 8, share).transpose(1, 0, 2).reshape(8, width).astype(F32)
    )
    up_bias_all = thin_all[:, 8 * share:].reshape(ff_total).astype(F32)
    gain1, shift1, bias_q, bias_v, bias_o, gain2, shift2, bias_d = [vectors[i] for i in range(8)]
    up_shift = lax.dynamic_slice_in_dim(up_bias_all, z * ff, ff)

    x_full = gather_z(inputs[0])
    cot, _ = lax.optimization_barrier((cotangent[0], x_full))
    g_full = gather_z(cot)

    cut = -(-share // 16) * 8
    chunks = []
    for lo, hi in ((0, cut), (cut, share)):
        raw = ring_z(qkv_weight[lo:hi]).transpose(1, 0, 2).reshape(hi - lo, 3 * width)
        wq_s = pad_cols(raw[:, :width], wide)
        wk_s = pad_cols(raw[:, width : 2 * width], wide)
        wv_s = pad_cols(raw[:, 2 * width :], wide)
        chunks.append(jnp.concatenate([wq_s, pair_up(wk_s, wv_s)], axis=1))
    qkv_full = gather_dp(chunks).reshape(width, 3 * wide)
    out_s, _ = lax.optimization_barrier((out_weight, chunks[1]))
    out_rows = ring_z(out_s).transpose(1, 0, 2).reshape(share, width)
    out_rows, up_s, down_s, qkv_full = lax.optimization_barrier((out_rows, up_weight, down_weight, qkv_full))
    wq = qkv_full[:, :wide]
    wkv = qkv_full[:, wide:]

    x_own = inputs[0].astype(F32)
    normed1, inv1 = ln_stats(x_own)
    attn_own = (normed1 * gain1 + shift1).astype(BF)
    normed1_full, _ = ln_stats(x_full.astype(F32))
    attn_full = (normed1_full * gain1 + shift1).astype(BF)
    q = (mm(attn_own, wq) + pad_cols(bias_q, wide)).astype(BF)
    bias_kv = pair_up(jnp.zeros((wide,), F32), pad_cols(bias_v, wide))
    kv = (mm(attn_full, wkv) + bias_kv).astype(BF)
    wo = gather_dp([out_rows]).reshape(width, width)
    mlp_w = gather_dp([jnp.concatenate([up_s, down_s.T], axis=1)]).reshape(width, 2 * ff)
    up_full = mlp_w[:, :ff]
    down_t = mlp_w[:, ff:]
    ctx, lse = attend(meta, q, kv)
    ctx, g_full = lax.optimization_barrier((ctx, g_full))
    ctx = ctx[:, :width]
    resid = x_own + mm(ctx, wo) + bias_o
    normed2, inv2 = ln_stats(resid)
    mlp_in = (normed2 * gain2 + shift2).astype(BF)
    mlp_full = gather_z(mlp_in)
    pre = mm(mlp_full, up_full) + up_shift
    act, slope = gelu_parts(pre)
    hidden = act.astype(BF)

    position = lax.broadcasted_iota(jnp.int32, (total_rows, 1), 0)
    g_full = g_full * (position < length).astype(BF)
    own_position = first + lax.broadcasted_iota(jnp.int32, (rows, 1), 0)
    grad_out = cotangent[0].astype(F32) * (own_position < length).astype(F32)
    grad_pre = mm(g_full, down_t) * slope
    grad_pre_b = grad_pre.astype(BF)
    grad_mlp = scatter_z(mm(grad_pre_b, up_full, NT).astype(BF))
    mlp_part, _ = lax.optimization_barrier((mm(hidden, down_t, NT).astype(BF), grad_mlp))
    mlp_out = scatter_z(mlp_part)
    up_b_block = jnp.sum(grad_pre, axis=0)
    mlp_dw = jnp.concatenate([mm(mlp_full, grad_pre_b, TN), mm(g_full, hidden, TN)], axis=1).astype(BF)
    grad_resid = grad_out + ln_back(grad_mlp, normed2, inv2, gain2)
    grad_resid_b = grad_resid.astype(BF)
    grad_ctx = pad_cols(mm(grad_resid_b, wo, NT).astype(BF), wide)
    dwo = scatter_dp(mm(ctx, grad_resid_b, TN).astype(BF).reshape(n, share, width))
    dq, dkv = attend_back(meta, q, kv, lse, grad_ctx)
    mlp_dw = scatter_dp(mlp_dw.reshape(n, share, 2 * ff))
    dq, dkv, mlp_out = lax.optimization_barrier((dq, dkv, mlp_out))
    outputs = (resid + mlp_out + bias_d).astype(BF)
    up_grad = mlp_dw[:, :ff]
    down_grad = mlp_dw[:, ff:].T
    dw = jnp.concatenate([mm(attn_own, dq, TN), mm(attn_full, dkv, TN)], axis=1).astype(BF)
    dq, dkv, dw = lax.optimization_barrier((dq, dkv, dw))
    dw = scatter_dp(dw.reshape(n, share, 3 * wide))
    part_kv = mm(dkv, wkv, NT)
    part_q = mm(dq, wq, NT)
    grad_attn = scatter_z(part_kv.astype(BF))

    dv_sum = pair_split(jnp.sum(dkv.astype(F32), axis=0))[1][:width]
    vec = jnp.stack(
        [
            jnp.sum(part_kv * normed1_full, axis=0) + jnp.sum(part_q * normed1, axis=0),
            jnp.sum(part_kv, axis=0) + jnp.sum(part_q, axis=0),
            jnp.sum(dq.astype(F32), axis=0)[:width],
            dv_sum,
            jnp.sum(grad_resid, axis=0),
            jnp.sum(grad_mlp * normed2, axis=0),
            jnp.sum(grad_mlp, axis=0),
            jnp.sum(grad_out, axis=0),
        ]
    )
    up_b = lax.dynamic_update_slice_in_dim(jnp.zeros((ff_total,), F32), up_b_block, z * ff, 0)
    thin_grad = jnp.concatenate(
        [vec.reshape(8, n, share).transpose(1, 0, 2).reshape(n, 8 * share), up_b.reshape(n, ff_total // n)],
        axis=1,
    )
    thin_len = thin_grad.shape[1]
    thin_grad = scatter_dp(thin_grad.astype(BF)[:, None, :])

    piece = qkv_cols + width // zs
    dwk, dwv = pair_split(dw[:, wide:])
    dw_cols = jnp.concatenate([dw[:, :width], dwk[:, :width], dwv[:, :width]], axis=1).astype(BF)
    dwo = dwo.astype(BF)
    extra = -(-thin_len // piece)
    thin_rows = pad_cols(thin_grad.astype(BF), extra * piece).reshape(extra, piece)
    lines = -(-(share + extra) // 16) * 16
    thin_rows = jnp.pad(thin_rows, [(0, lines - share - extra), (0, 0)])
    blocks = []
    for j in range(zs):
        blocks.append(
            jnp.concatenate(
                [
                    dw_cols[:, j * qkv_cols : (j + 1) * qkv_cols],
                    dwo[:, j * (width // zs) : (j + 1) * (width // zs)],
                ],
                axis=1,
            )
        )
        blocks.append(thin_rows)
    last, grad_attn = lax.optimization_barrier((jnp.concatenate(blocks, axis=0), grad_attn))
    last = scatter_z(last)
    input_grad = grad_resid + ln_back(grad_attn + part_q, normed1, inv1, gain1)
    attn_dw = last[:share]
    thin_grad = last[share : share + extra].reshape(extra * piece)[:thin_len]
    vec_out = thin_grad[: 8 * share].reshape(8, share)
    return (
        outputs[None],
        input_grad[None],
        vec_out[0],
        vec_out[1],
        attn_dw[:, :qkv_cols],
        vec_out[2],
        vec_out[3],
        attn_dw[:, qkv_cols:],
        vec_out[4],
        vec_out[5],
        vec_out[6],
        up_grad,
        thin_grad[8 * share:],
        down_grad,
        vec_out[7],
    )


def solution(mesh):
    row = P("dp", "seq", None)
    vec = P("dp")
    mat = P("dp", "seq")
    in_specs = (row, vec, row, vec, vec, mat, vec, vec, mat, vec, vec, vec, mat, vec, P("seq", "dp"), vec)
    out_specs = (row, row, vec, vec, mat, vec, vec, mat, vec, vec, vec, mat, vec, P("seq", "dp"), vec)

    return jax.shard_map(shards, mesh=mesh, in_specs=in_specs, out_specs=out_specs, check_vma=False)
```

```python
import jax
import jax.numpy as jnp
from jax import lax
from jax.experimental import pallas as pl
from jax.experimental.pallas import tpu as pltpu
from jax.sharding import PartitionSpec as P


HD = 64
LANES = 128
EPS = 1e-05
GELU_C = 0.7978845608028654
MASKED = -1e30
BF = jnp.bfloat16
F32 = jnp.float32


def mm(a, b, dims=((1,), (0,))):
    return lax.dot_general(a, b, (dims, ((), ())), preferred_element_type=F32)


NT = ((1,), (1,))
TN = ((0,), (0,))


def ln_stats(x):
    average = jnp.mean(x, axis=-1, keepdims=True)
    centered = x - average
    variance = jnp.mean(centered * centered, axis=-1, keepdims=True)
    inv = lax.rsqrt(variance + EPS)
    return centered * inv, inv


def ln_back(grad_in, normed, inv, gain):
    scaled = grad_in * gain
    return inv * (
        scaled
        - jnp.mean(scaled, axis=-1, keepdims=True)
        - normed * jnp.mean(scaled * normed, axis=-1, keepdims=True)
    )


def gelu_parts(pre):
    tangent = jnp.tanh(GELU_C * (pre + 0.044715 * pre * pre * pre))
    result = 0.5 * pre * (1.0 + tangent)
    slope = 0.5 * (1.0 + tangent) + 0.5 * pre * (1.0 - tangent * tangent) * GELU_C * (
        1.0 + 3.0 * 0.044715 * pre * pre
    )
    return result, slope


def head_mask(rows, which):
    lane = lax.broadcasted_iota(jnp.int32, (rows, LANES), 1)
    return (lane >= HD) if which else (lane < HD)


def fill_mask(meta, mask_ref):
    key = lax.broadcasted_iota(jnp.int32, mask_ref.shape, 0)
    row = lax.broadcasted_iota(jnp.int32, mask_ref.shape, 1) + meta[0]
    mask_ref[...] = jnp.where((key <= row) & (key < meta[1]), 0.0, MASKED)


def attend_kernel(meta, q_ref, kv_ref, ctx_ref, lse_ref, mask_ref):
    rows = q_ref.shape[0]

    @pl.when(pl.program_id(0) == 0)
    def _():
        fill_mask(meta, mask_ref)

    k = kv_ref[:, :LANES]
    vt = kv_ref[:, LANES:].T
    q = q_ref[...] * jnp.asarray(HD ** -0.5, BF)
    pieces = []
    for which in range(2):
        qm = jnp.where(head_mask(rows, which), q, jnp.zeros_like(q))
        s = mm(k, qm, NT) + mask_ref[...]
        top = jnp.max(s, axis=0, keepdims=True)
        e = jnp.exp(s - top)
        total = jnp.sum(e, axis=0, keepdims=True)
        weights = (e * (1.0 / total)).astype(BF)
        pieces.append(mm(vt[which * HD:(which + 1) * HD], weights))
        lse_ref[0, which:which + 1, :] = top + jnp.log(total)
    ctx_ref[...] = jnp.concatenate(pieces, axis=0).T.astype(BF)


def attend(meta, q, kv):
    rows, width = q.shape
    keys = kv.shape[0]
    pairs = width // LANES
    return pl.pallas_call(
        attend_kernel,
        grid_spec=pltpu.PrefetchScalarGridSpec(
            num_scalar_prefetch=1,
            grid=(pairs,),
            in_specs=[
                pl.BlockSpec((rows, LANES), lambda p, m: (0, p)),
                pl.BlockSpec((keys, 2 * LANES), lambda p, m: (0, p)),
            ],
            out_specs=[
                pl.BlockSpec((rows, LANES), lambda p, m: (0, p)),
                pl.BlockSpec((1, 2, rows), lambda p, m: (p, 0, 0)),
            ],
            scratch_shapes=[pltpu.VMEM((keys, rows), F32)],
        ),
        out_shape=[
            jax.ShapeDtypeStruct((rows, width), BF),
            jax.ShapeDtypeStruct((pairs, 2, rows), F32),
        ],
        cost_estimate=pl.CostEstimate(
            flops=8 * rows * keys * width, transcendentals=2 * pairs * rows * keys, bytes_accessed=6 * keys * width
        ),
        name="attend",
    )(meta, q, kv)


def attend_back_kernel(meta, q_ref, kv_ref, lse_ref, g_ref, dq_ref, dkv_ref, mask_ref):
    rows = q_ref.shape[0]

    @pl.when(pl.program_id(0) == 0)
    def _():
        fill_mask(meta, mask_ref)

    scale = jnp.asarray(HD ** -0.5, BF)
    k = kv_ref[:, :LANES]
    v = kv_ref[:, LANES:]
    kt = k.T
    q = q_ref[...]
    g = g_ref[...]
    dq, weights_all, ds_all, q_all, g_all = [], [], [], [], []
    for which in range(2):
        mask = head_mask(rows, which)
        qm = jnp.where(mask, q, jnp.zeros_like(q))
        gm = jnp.where(mask, g, jnp.zeros_like(g))
        s = mm(k, qm * scale, NT) + mask_ref[...]
        weights = jnp.exp(s - lse_ref[0, which:which + 1, :])
        dprob = mm(v, gm * scale, NT)
        delta = jnp.sum(weights * dprob, axis=0, keepdims=True)
        ds = (weights * (dprob - delta)).astype(BF)
        dq.append(mm(kt[which * HD:(which + 1) * HD], ds))
        weights_all.append(weights.astype(BF))
        ds_all.append(ds)
        q_all.append(qm)
        g_all.append(gm)
    dq_ref[...] = jnp.concatenate(dq, axis=0).T.astype(BF)
    dk = mm(jnp.concatenate(ds_all, axis=1), jnp.concatenate(q_all, axis=0))
    dv = mm(jnp.concatenate(weights_all, axis=1), jnp.concatenate(g_all, axis=0))
    dkv_ref[:, :LANES] = dk.astype(BF)
    dkv_ref[:, LANES:] = dv.astype(BF)


def attend_back(meta, q, kv, lse, g):
    rows, width = q.shape
    keys = kv.shape[0]
    pairs = width // LANES
    return pl.pallas_call(
        attend_back_kernel,
        grid_spec=pltpu.PrefetchScalarGridSpec(
            num_scalar_prefetch=1,
            grid=(pairs,),
            in_specs=[
                pl.BlockSpec((rows, LANES), lambda p, m: (0, p)),
                pl.BlockSpec((keys, 2 * LANES), lambda p, m: (0, p)),
                pl.BlockSpec((1, 2, rows), lambda p, m: (p, 0, 0)),
                pl.BlockSpec((rows, LANES), lambda p, m: (0, p)),
            ],
            out_specs=[
                pl.BlockSpec((rows, LANES), lambda p, m: (0, p)),
                pl.BlockSpec((keys, 2 * LANES), lambda p, m: (0, p)),
            ],
            scratch_shapes=[pltpu.VMEM((keys, rows), F32)],
        ),
        out_shape=[
            jax.ShapeDtypeStruct((rows, width), BF),
            jax.ShapeDtypeStruct((keys, 2 * width), BF),
        ],
        cost_estimate=pl.CostEstimate(
            flops=20 * rows * keys * width, transcendentals=2 * pairs * rows * keys, bytes_accessed=12 * keys * width
        ),
        name="attend_back",
    )(meta, q, kv, lse, g)


def swap(x, bit):
    n = lax.axis_size("dp")
    return lax.ppermute(x, "dp", [(i, i ^ bit) for i in range(n)])


def ring_z(x):
    size = lax.axis_size("seq")
    me = lax.axis_index("seq")
    parts = [x]
    for d in range(1, size):
        parts.append(lax.ppermute(x, "seq", [(i, (i + d) % size) for i in range(size)]))
    blocks = []
    for j in range(size):
        block = parts[0]
        for d in range(1, size):
            block = jnp.where((me - j) % size == d, parts[d], block)
        blocks.append(block)
    return blocks


def place_kernel(meta, *refs):
    pieces, out, sems = refs[:-2], refs[-2], refs[-1]
    count = out.shape[0]
    copies = []
    at = 0
    for c in range(len(pieces) // count):
        rows = pieces[c * count].shape[0]
        for e in range(count):
            piece = pieces[c * count + e]
            spot = out.at[meta[0] ^ e, pl.ds(at, rows), :]
            copies.append(pltpu.make_async_copy(piece, spot, sems.at[c * count + e]))
        at += rows
    for copy in copies:
        copy.start()
    for copy in copies:
        copy.wait()


def place(me, pieces, count, rows):
    return pl.pallas_call(
        place_kernel,
        grid_spec=pltpu.PrefetchScalarGridSpec(
            num_scalar_prefetch=1,
            grid=(1,),
            in_specs=[pl.BlockSpec(memory_space=pl.ANY)] * len(pieces),
            out_specs=pl.BlockSpec(memory_space=pl.ANY),
            scratch_shapes=[pltpu.SemaphoreType.DMA((len(pieces),))],
        ),
        out_shape=jax.ShapeDtypeStruct((count, rows, pieces[0].shape[1]), pieces[0].dtype),
        name="place",
    )(me.reshape(1).astype(jnp.int32), *pieces)


def gather_dp(chunks):
    n = lax.axis_size("dp")
    if n != 8:
        return lax.all_gather(jnp.concatenate(chunks, axis=0), "dp", axis=0)
    pieces = []
    for x in chunks:
        for d in range(n // 2):
            got = swap(x, 2 * d) if d else x
            pieces += [got, swap(got, 1)]
    return place(lax.axis_index("dp"), pieces, n, sum(x.shape[0] for x in chunks))


def scatter_dp(g):
    n = lax.axis_size("dp")
    if n != 8:
        return lax.psum_scatter(g, "dp", scatter_dimension=0).astype(F32)
    me = lax.axis_index("dp")
    group, core = me // 2, me % 2
    pairs = g.reshape((n // 2, 2) + g.shape[1:])
    keep = lax.dynamic_index_in_dim(pairs, core, 1, keepdims=False)
    send = lax.dynamic_index_in_dim(pairs, 1 - core, 1, keepdims=False)
    got = swap(send, 1)
    summed = (keep.astype(F32) + got.astype(F32)).astype(BF)
    total = lax.dynamic_index_in_dim(summed, group, 0, keepdims=False).astype(F32)
    for d in range(1, n // 2):
        part = lax.dynamic_index_in_dim(summed, group ^ d, 0, keepdims=False)
        total = total + swap(part, 2 * d).astype(F32)
    return total


def gather_z(x):
    return lax.all_gather(x, "seq", axis=0, tiled=True)


def scatter_z(x):
    return lax.psum_scatter(x, "seq", scatter_dimension=0, tiled=True).astype(F32)


def pad_cols(x, width):
    return jnp.pad(x, [(0, 0)] * (x.ndim - 1) + [(0, width - x.shape[-1])])


def pair_up(a, b):
    lead = a.shape[:-1]
    blocks = a.shape[-1] // LANES
    both = jnp.stack([a.reshape(lead + (blocks, LANES)), b.reshape(lead + (blocks, LANES))], axis=-2)
    return both.reshape(lead + (2 * a.shape[-1],))


def pair_split(x):
    lead = x.shape[:-1]
    both = x.reshape(lead + (x.shape[-1] // (2 * LANES), 2, LANES))
    half = lead + (x.shape[-1] // 2,)
    return both[..., 0, :].reshape(half), both[..., 1, :].reshape(half)


def shards(
    inputs,
    lengths,
    cotangent,
    norm1_gain,
    norm1_bias,
    qkv_weight,
    query_bias,
    value_bias,
    out_weight,
    out_bias,
    norm2_gain,
    norm2_bias,
    up_weight,
    up_bias,
    down_weight,
    down_bias,
):
    n = lax.axis_size("dp")
    zs = lax.axis_size("seq")
    z = lax.axis_index("seq")
    rows, width = inputs.shape[1:]
    total_rows = rows * zs
    share = norm1_gain.shape[0]
    wide = -(-width // LANES) * LANES
    qkv_cols = qkv_weight.shape[1]
    ff = up_weight.shape[1]
    ff_total = ff * zs
    length = lengths[0]
    first = z * rows
    meta = jnp.stack([first, length]).astype(jnp.int32)

    thin = jnp.stack(
        [norm1_gain, norm1_bias, query_bias, value_bias, out_bias, norm2_gain, norm2_bias, down_bias]
    ).reshape(1, 8 * share)
    thin_all = gather_dp([jnp.concatenate([thin, up_bias.reshape(1, -1)], axis=1)])
    thin_all = thin_all.reshape(n, 8 * share + up_bias.shape[0])
    vectors = (
        thin_all[:, : 8 * share].reshape(n, 8, share).transpose(1, 0, 2).reshape(8, width).astype(F32)
    )
    up_bias_all = thin_all[:, 8 * share:].reshape(ff_total).astype(F32)
    gain1, shift1, bias_q, bias_v, bias_o, gain2, shift2, bias_d = [vectors[i] for i in range(8)]
    up_shift = lax.dynamic_slice_in_dim(up_bias_all, z * ff, ff)

    x_full = gather_z(inputs[0])
    cot, _ = lax.optimization_barrier((cotangent[0], x_full))
    g_full = gather_z(cot)

    cut = -(-share // 16) * 8
    chunks = []
    for lo, hi in ((0, cut), (cut, share)):
        raw = jnp.concatenate(ring_z(qkv_weight[lo:hi]), axis=1)
        wq_s = pad_cols(raw[:, :width], wide)
        wk_s = pad_cols(raw[:, width : 2 * width], wide)
        wv_s = pad_cols(raw[:, 2 * width :], wide)
        chunks.append(jnp.concatenate([wq_s, pair_up(wk_s, wv_s)], axis=1))
    qkv_full = gather_dp(chunks).reshape(width, 3 * wide)
    out_rows = jnp.concatenate(ring_z(out_weight), axis=1)
    out_rows, up_s, down_s, qkv_full = lax.optimization_barrier((out_rows, up_weight, down_weight, qkv_full))
    wq = qkv_full[:, :wide]
    wkv = qkv_full[:, wide:]

    x_own = inputs[0].astype(F32)
    normed1, inv1 = ln_stats(x_own)
    attn_own = (normed1 * gain1 + shift1).astype(BF)
    normed1_full, _ = ln_stats(x_full.astype(F32))
    attn_full = (normed1_full * gain1 + shift1).astype(BF)
    q = (mm(attn_own, wq) + pad_cols(bias_q, wide)).astype(BF)
    bias_kv = pair_up(jnp.zeros((wide,), F32), pad_cols(bias_v, wide))
    kv = (mm(attn_full, wkv) + bias_kv).astype(BF)
    wo = gather_dp([out_rows]).reshape(width, width)
    mlp_w = gather_dp([jnp.concatenate([up_s, down_s.T], axis=1)]).reshape(width, 2 * ff)
    up_full = mlp_w[:, :ff]
    down_t = mlp_w[:, ff:]
    ctx, lse = attend(meta, q, kv)
    ctx, g_full = lax.optimization_barrier((ctx, g_full))
    ctx = ctx[:, :width]
    resid = x_own + mm(ctx, wo) + bias_o
    normed2, inv2 = ln_stats(resid)
    mlp_in = (normed2 * gain2 + shift2).astype(BF)
    mlp_full = gather_z(mlp_in)
    pre = mm(mlp_full, up_full) + up_shift
    act, slope = gelu_parts(pre)
    hidden = act.astype(BF)

    position = lax.broadcasted_iota(jnp.int32, (total_rows, 1), 0)
    g_full = g_full * (position < length).astype(BF)
    own_position = first + lax.broadcasted_iota(jnp.int32, (rows, 1), 0)
    grad_out = cotangent[0].astype(F32) * (own_position < length).astype(F32)
    grad_pre = mm(g_full, down_t) * slope
    grad_pre_b = grad_pre.astype(BF)
    grad_mlp = scatter_z(mm(grad_pre_b, up_full, NT).astype(BF))
    mlp_part, _ = lax.optimization_barrier((mm(hidden, down_t, NT).astype(BF), grad_mlp))
    mlp_out = scatter_z(mlp_part)
    up_b_block = jnp.sum(grad_pre, axis=0)
    mlp_dw = jnp.concatenate([mm(mlp_full, grad_pre_b, TN), mm(g_full, hidden, TN)], axis=1).astype(BF)
    grad_resid = grad_out + ln_back(grad_mlp, normed2, inv2, gain2)
    grad_resid_b = grad_resid.astype(BF)
    grad_ctx = pad_cols(mm(grad_resid_b, wo, NT).astype(BF), wide)
    dwo = scatter_dp(mm(ctx, grad_resid_b, TN).astype(BF).reshape(n, share, width))
    dq, dkv = attend_back(meta, q, kv, lse, grad_ctx)
    mlp_dw = scatter_dp(mlp_dw.reshape(n, share, 2 * ff))
    dq, dkv, mlp_out = lax.optimization_barrier((dq, dkv, mlp_out))
    outputs = (resid + mlp_out + bias_d).astype(BF)
    up_grad = mlp_dw[:, :ff]
    down_grad = mlp_dw[:, ff:].T
    dw = jnp.concatenate([mm(attn_own, dq, TN), mm(attn_full, dkv, TN)], axis=1).astype(BF)
    dq, dkv, dw = lax.optimization_barrier((dq, dkv, dw))
    dw = dw.reshape(n, share, 3 * wide)
    dw_parts = [scatter_dp(dw[:, :cut]), scatter_dp(dw[:, cut:])]
    part_kv = mm(dkv, wkv, NT)
    part_q = mm(dq, wq, NT)
    grad_attn = scatter_z(part_kv.astype(BF))

    dv_sum = pair_split(jnp.sum(dkv.astype(F32), axis=0))[1][:width]
    vec = jnp.stack(
        [
            jnp.sum(part_kv * normed1_full, axis=0) + jnp.sum(part_q * normed1, axis=0),
            jnp.sum(part_kv, axis=0) + jnp.sum(part_q, axis=0),
            jnp.sum(dq.astype(F32), axis=0)[:width],
            dv_sum,
            jnp.sum(grad_resid, axis=0),
            jnp.sum(grad_mlp * normed2, axis=0),
            jnp.sum(grad_mlp, axis=0),
            jnp.sum(grad_out, axis=0),
        ]
    )
    up_b = lax.dynamic_update_slice_in_dim(jnp.zeros((ff_total,), F32), up_b_block, z * ff, 0)
    thin_grad = jnp.concatenate(
        [vec.reshape(8, n, share).transpose(1, 0, 2).reshape(n, 8 * share), up_b.reshape(n, ff_total // n)],
        axis=1,
    )
    thin_len = thin_grad.shape[1]
    thin_grad = scatter_dp(thin_grad.astype(BF)[:, None, :])

    piece = qkv_cols + width // zs
    dwo = dwo.astype(BF)
    extra = -(-thin_len // piece)
    thin_rows = pad_cols(thin_grad.astype(BF), extra * piece).reshape(extra, piece)
    sums = []
    for part, lo, hi in ((dw_parts[0], 0, cut), (dw_parts[1], cut, share)):
        part = part.astype(BF)
        dwk, dwv = pair_split(part[:, wide:])
        cols = jnp.concatenate([part[:, :width], dwk[:, :width], dwv[:, :width]], axis=1)
        blocks = []
        for j in range(zs):
            out_part = dwo[lo:hi, j * (width // zs) : (j + 1) * (width // zs)]
            blocks.append(jnp.concatenate([cols[:, j * qkv_cols : (j + 1) * qkv_cols], out_part], axis=1))
            if lo:
                lines = -(-(hi - lo + extra) // 16) * 16
                blocks.append(jnp.pad(thin_rows, [(0, lines - (hi - lo) - extra), (0, 0)]))
        block = jnp.concatenate(blocks, axis=0)
        if lo:
            block, grad_attn = lax.optimization_barrier((block, grad_attn))
        sums.append(scatter_z(block))
    input_grad = grad_resid + ln_back(grad_attn + part_q, normed1, inv1, gain1)
    attn_dw = jnp.concatenate([sums[0], sums[1][: share - cut]], axis=0)
    thin_grad = sums[1][share - cut : share - cut + extra].reshape(extra * piece)[:thin_len]
    vec_out = thin_grad[: 8 * share].reshape(8, share)
    return (
        outputs[None],
        input_grad[None],
        vec_out[0],
        vec_out[1],
        attn_dw[:, :qkv_cols],
        vec_out[2],
        vec_out[3],
        attn_dw[:, qkv_cols:],
        vec_out[4],
        vec_out[5],
        vec_out[6],
        up_grad,
        thin_grad[8 * share:],
        down_grad,
        vec_out[7],
    )


def solution(mesh):
    row = P("dp", "seq", None)
    vec = P("dp")
    mat = P("dp", "seq")
    in_specs = (row, vec, row, vec, vec, mat, vec, vec, mat, vec, vec, vec, mat, vec, P("seq", "dp"), vec)
    out_specs = (row, row, vec, vec, mat, vec, vec, mat, vec, vec, vec, mat, vec, P("seq", "dp"), vec)

    return jax.shard_map(shards, mesh=mesh, in_specs=in_specs, out_specs=out_specs, check_vma=False)
```

```python
import jax
import jax.numpy as jnp
from jax import lax
from jax.experimental import pallas as pl
from jax.experimental.pallas import tpu as pltpu
from jax.sharding import PartitionSpec as P


HD = 64
LANES = 128
EPS = 1e-05
GELU_C = 0.7978845608028654
MASKED = -1e30
BF = jnp.bfloat16
F32 = jnp.float32


def mm(a, b, dims=((1,), (0,))):
    return lax.dot_general(a, b, (dims, ((), ())), preferred_element_type=F32)


NT = ((1,), (1,))
TN = ((0,), (0,))


def ln_stats(x):
    average = jnp.mean(x, axis=-1, keepdims=True)
    centered = x - average
    variance = jnp.mean(centered * centered, axis=-1, keepdims=True)
    inv = lax.rsqrt(variance + EPS)
    return centered * inv, inv


def ln_back(grad_in, normed, inv, gain):
    scaled = grad_in * gain
    return inv * (
        scaled
        - jnp.mean(scaled, axis=-1, keepdims=True)
        - normed * jnp.mean(scaled * normed, axis=-1, keepdims=True)
    )


def gelu_parts(pre):
    tangent = jnp.tanh(GELU_C * (pre + 0.044715 * pre * pre * pre))
    result = 0.5 * pre * (1.0 + tangent)
    slope = 0.5 * (1.0 + tangent) + 0.5 * pre * (1.0 - tangent * tangent) * GELU_C * (
        1.0 + 3.0 * 0.044715 * pre * pre
    )
    return result, slope


def head_mask(rows, which):
    lane = lax.broadcasted_iota(jnp.int32, (rows, LANES), 1)
    return (lane >= HD) if which else (lane < HD)


def fill_mask(meta, mask_ref):
    key = lax.broadcasted_iota(jnp.int32, mask_ref.shape, 0)
    row = lax.broadcasted_iota(jnp.int32, mask_ref.shape, 1) + meta[0]
    mask_ref[...] = jnp.where((key <= row) & (key < meta[1]), 0.0, MASKED)


def attend_kernel(meta, q_ref, kv_ref, ctx_ref, lse_ref, mask_ref):
    rows = q_ref.shape[0]

    @pl.when(pl.program_id(0) == 0)
    def _():
        fill_mask(meta, mask_ref)

    k = kv_ref[:, :LANES]
    vt = kv_ref[:, LANES:].T
    q = q_ref[...] * jnp.asarray(HD ** -0.5, BF)
    pieces = []
    for which in range(2):
        qm = jnp.where(head_mask(rows, which), q, jnp.zeros_like(q))
        s = mm(k, qm, NT) + mask_ref[...]
        top = jnp.max(s, axis=0, keepdims=True)
        e = jnp.exp(s - top)
        total = jnp.sum(e, axis=0, keepdims=True)
        weights = (e * (1.0 / total)).astype(BF)
        pieces.append(mm(vt[which * HD:(which + 1) * HD], weights))
        lse_ref[0, which:which + 1, :] = top + jnp.log(total)
    ctx_ref[...] = jnp.concatenate(pieces, axis=0).T.astype(BF)


def attend(meta, q, kv):
    rows, width = q.shape
    keys = kv.shape[0]
    pairs = width // LANES
    return pl.pallas_call(
        attend_kernel,
        grid_spec=pltpu.PrefetchScalarGridSpec(
            num_scalar_prefetch=1,
            grid=(pairs,),
            in_specs=[
                pl.BlockSpec((rows, LANES), lambda p, m: (0, p)),
                pl.BlockSpec((keys, 2 * LANES), lambda p, m: (0, p)),
            ],
            out_specs=[
                pl.BlockSpec((rows, LANES), lambda p, m: (0, p)),
                pl.BlockSpec((1, 2, rows), lambda p, m: (p, 0, 0)),
            ],
            scratch_shapes=[pltpu.VMEM((keys, rows), F32)],
        ),
        out_shape=[
            jax.ShapeDtypeStruct((rows, width), BF),
            jax.ShapeDtypeStruct((pairs, 2, rows), F32),
        ],
        cost_estimate=pl.CostEstimate(
            flops=8 * rows * keys * width, transcendentals=2 * pairs * rows * keys, bytes_accessed=6 * keys * width
        ),
        name="attend",
    )(meta, q, kv)


def attend_back_kernel(meta, q_ref, kv_ref, lse_ref, g_ref, dq_ref, dkv_ref, mask_ref):
    rows = q_ref.shape[0]

    @pl.when(pl.program_id(0) == 0)
    def _():
        fill_mask(meta, mask_ref)

    scale = jnp.asarray(HD ** -0.5, BF)
    k = kv_ref[:, :LANES]
    v = kv_ref[:, LANES:]
    kt = k.T
    q = q_ref[...]
    g = g_ref[...]
    dq, weights_all, ds_all, q_all, g_all = [], [], [], [], []
    for which in range(2):
        mask = head_mask(rows, which)
        qm = jnp.where(mask, q, jnp.zeros_like(q))
        gm = jnp.where(mask, g, jnp.zeros_like(g))
        s = mm(k, qm * scale, NT) + mask_ref[...]
        weights = jnp.exp(s - lse_ref[0, which:which + 1, :])
        dprob = mm(v, gm * scale, NT)
        delta = jnp.sum(weights * dprob, axis=0, keepdims=True)
        ds = (weights * (dprob - delta)).astype(BF)
        dq.append(mm(kt[which * HD:(which + 1) * HD], ds))
        weights_all.append(weights.astype(BF))
        ds_all.append(ds)
        q_all.append(qm)
        g_all.append(gm)
    dq_ref[...] = jnp.concatenate(dq, axis=0).T.astype(BF)
    dk = mm(jnp.concatenate(ds_all, axis=1), jnp.concatenate(q_all, axis=0))
    dv = mm(jnp.concatenate(weights_all, axis=1), jnp.concatenate(g_all, axis=0))
    dkv_ref[:, :LANES] = dk.astype(BF)
    dkv_ref[:, LANES:] = dv.astype(BF)


def attend_back(meta, q, kv, lse, g):
    rows, width = q.shape
    keys = kv.shape[0]
    pairs = width // LANES
    return pl.pallas_call(
        attend_back_kernel,
        grid_spec=pltpu.PrefetchScalarGridSpec(
            num_scalar_prefetch=1,
            grid=(pairs,),
            in_specs=[
                pl.BlockSpec((rows, LANES), lambda p, m: (0, p)),
                pl.BlockSpec((keys, 2 * LANES), lambda p, m: (0, p)),
                pl.BlockSpec((1, 2, rows), lambda p, m: (p, 0, 0)),
                pl.BlockSpec((rows, LANES), lambda p, m: (0, p)),
            ],
            out_specs=[
                pl.BlockSpec((rows, LANES), lambda p, m: (0, p)),
                pl.BlockSpec((keys, 2 * LANES), lambda p, m: (0, p)),
            ],
            scratch_shapes=[pltpu.VMEM((keys, rows), F32)],
        ),
        out_shape=[
            jax.ShapeDtypeStruct((rows, width), BF),
            jax.ShapeDtypeStruct((keys, 2 * width), BF),
        ],
        cost_estimate=pl.CostEstimate(
            flops=20 * rows * keys * width, transcendentals=2 * pairs * rows * keys, bytes_accessed=12 * keys * width
        ),
        name="attend_back",
    )(meta, q, kv, lse, g)


def swap(x, bit):
    n = lax.axis_size("dp")
    return lax.ppermute(x, "dp", [(i, i ^ bit) for i in range(n)])


def ring_z(x):
    size = lax.axis_size("seq")
    me = lax.axis_index("seq")
    parts = [x]
    for d in range(1, size):
        parts.append(lax.ppermute(x, "seq", [(i, (i + d) % size) for i in range(size)]))
    blocks = []
    for j in range(size):
        block = parts[0]
        for d in range(1, size):
            block = jnp.where((me - j) % size == d, parts[d], block)
        blocks.append(block)
    return blocks


def place_kernel(meta, *refs):
    pieces, out, sems = refs[:-2], refs[-2], refs[-1]
    count = out.shape[0]
    copies = []
    at = 0
    for c in range(len(pieces) // count):
        rows = pieces[c * count].shape[0]
        for e in range(count):
            piece = pieces[c * count + e]
            spot = out.at[meta[0] ^ e, pl.ds(at, rows), :]
            copies.append(pltpu.make_async_copy(piece, spot, sems.at[c * count + e]))
        at += rows
    for copy in copies:
        copy.start()
    for copy in copies:
        copy.wait()


def place(me, pieces, count, rows):
    return pl.pallas_call(
        place_kernel,
        grid_spec=pltpu.PrefetchScalarGridSpec(
            num_scalar_prefetch=1,
            grid=(1,),
            in_specs=[pl.BlockSpec(memory_space=pltpu.VMEM)] * len(pieces),
            out_specs=pl.BlockSpec(memory_space=pl.ANY),
            scratch_shapes=[pltpu.SemaphoreType.DMA((len(pieces),))],
        ),
        out_shape=jax.ShapeDtypeStruct((count, rows, pieces[0].shape[1]), pieces[0].dtype),
        name="place",
    )(me.reshape(1).astype(jnp.int32), *pieces)


def gather_dp(chunks):
    n = lax.axis_size("dp")
    if n != 8:
        return lax.all_gather(jnp.concatenate(chunks, axis=0), "dp", axis=0)
    pieces = []
    for x in chunks:
        for d in range(n // 2):
            got = swap(x, 2 * d) if d else x
            pieces += [got, swap(got, 1)]
    return place(lax.axis_index("dp"), pieces, n, sum(x.shape[0] for x in chunks))


def core_half(grads, mine):
    n = lax.axis_size("dp")
    core = lax.axis_index("dp") % 2
    which = core if mine else 1 - core
    cut_out = [
        lax.dynamic_index_in_dim(g.reshape((n // 2, 2) + g.shape[1:]), which, 1, keepdims=False) for g in grads
    ]
    return jnp.concatenate(cut_out, axis=2)


def scatter_dp(grads, send=None):
    n = lax.axis_size("dp")
    if n != 8:
        return lax.psum_scatter(jnp.concatenate(grads, axis=2), "dp", scatter_dimension=0).astype(F32)
    group = lax.axis_index("dp") // 2
    got = swap(core_half(grads, False) if send is None else send, 1)
    summed = (core_half(grads, True).astype(F32) + got.astype(F32)).astype(BF)
    total = lax.dynamic_index_in_dim(summed, group, 0, keepdims=False).astype(F32)
    for d in range(1, n // 2):
        part = lax.dynamic_index_in_dim(summed, group ^ d, 0, keepdims=False)
        total = total + swap(part, 2 * d).astype(F32)
    return total


def gather_z(x):
    return lax.all_gather(x, "seq", axis=0, tiled=True)


def scatter_z(x):
    return lax.psum_scatter(x, "seq", scatter_dimension=0, tiled=True).astype(F32)


def pad_cols(x, width):
    return jnp.pad(x, [(0, 0)] * (x.ndim - 1) + [(0, width - x.shape[-1])])


def pair_up(a, b):
    lead = a.shape[:-1]
    blocks = a.shape[-1] // LANES
    both = jnp.stack([a.reshape(lead + (blocks, LANES)), b.reshape(lead + (blocks, LANES))], axis=-2)
    return both.reshape(lead + (2 * a.shape[-1],))


def pair_split(x):
    lead = x.shape[:-1]
    both = x.reshape(lead + (x.shape[-1] // (2 * LANES), 2, LANES))
    half = lead + (x.shape[-1] // 2,)
    return both[..., 0, :].reshape(half), both[..., 1, :].reshape(half)


def shards(
    inputs,
    lengths,
    cotangent,
    norm1_gain,
    norm1_bias,
    qkv_weight,
    query_bias,
    value_bias,
    out_weight,
    out_bias,
    norm2_gain,
    norm2_bias,
    up_weight,
    up_bias,
    down_weight,
    down_bias,
):
    n = lax.axis_size("dp")
    zs = lax.axis_size("seq")
    z = lax.axis_index("seq")
    rows, width = inputs.shape[1:]
    total_rows = rows * zs
    share = norm1_gain.shape[0]
    wide = -(-width // LANES) * LANES
    qkv_cols = qkv_weight.shape[1]
    ff = up_weight.shape[1]
    ff_total = ff * zs
    length = lengths[0]
    first = z * rows
    meta = jnp.stack([first, length]).astype(jnp.int32)

    thin = jnp.stack(
        [norm1_gain, norm1_bias, query_bias, value_bias, out_bias, norm2_gain, norm2_bias, down_bias]
    ).reshape(1, 8 * share)
    thin_all = gather_dp([jnp.concatenate([thin, up_bias.reshape(1, -1)], axis=1)])
    thin_all = thin_all.reshape(n, 8 * share + up_bias.shape[0])
    cut = -(-share // 16) * 8
    raw = ring_z(qkv_weight)
    raw, own_x, thin_all = lax.optimization_barrier((raw, inputs[0], thin_all))
    vectors = (
        thin_all[:, : 8 * share].reshape(n, 8, share).transpose(1, 0, 2).reshape(8, width).astype(F32)
    )
    up_bias_all = thin_all[:, 8 * share:].reshape(ff_total).astype(F32)
    gain1, shift1, bias_q, bias_v, bias_o, gain2, shift2, bias_d = [vectors[i] for i in range(8)]
    up_shift = lax.dynamic_slice_in_dim(up_bias_all, z * ff, ff)
    x_full = gather_z(own_x)
    cot, _ = lax.optimization_barrier((cotangent[0], x_full))
    g_full = gather_z(cot)
    raw = jnp.concatenate(raw, axis=1)
    wq_s = pad_cols(raw[:, :width], wide)
    wk_s = pad_cols(raw[:, width : 2 * width], wide)
    wv_s = pad_cols(raw[:, 2 * width :], wide)
    qkv_s = jnp.concatenate([wq_s, pair_up(wk_s, wv_s)], axis=1)
    qkv_full = gather_dp([qkv_s]).reshape(width, 3 * wide)
    out_rows = jnp.concatenate(ring_z(out_weight), axis=1)
    out_rows, up_s, down_s, qkv_full = lax.optimization_barrier((out_rows, up_weight, down_weight, qkv_full))
    wq = qkv_full[:, :wide]
    wkv = qkv_full[:, wide:]

    x_own = inputs[0].astype(F32)
    normed1, inv1 = ln_stats(x_own)
    attn_own = (normed1 * gain1 + shift1).astype(BF)
    normed1_full, _ = ln_stats(x_full.astype(F32))
    attn_full = (normed1_full * gain1 + shift1).astype(BF)
    q = (mm(attn_own, wq) + pad_cols(bias_q, wide)).astype(BF)
    bias_kv = pair_up(jnp.zeros((wide,), F32), pad_cols(bias_v, wide))
    kv = (mm(attn_full, wkv) + bias_kv).astype(BF)
    wo = gather_dp([out_rows]).reshape(width, width)
    mlp_w = gather_dp([jnp.concatenate([up_s, down_s.T], axis=1)]).reshape(width, 2 * ff)
    up_full = mlp_w[:, :ff]
    down_t = mlp_w[:, ff:]
    ctx, lse = attend(meta, q, kv)
    ctx, g_full = lax.optimization_barrier((ctx, g_full))
    ctx = ctx[:, :width]
    resid = x_own + mm(ctx, wo) + bias_o
    normed2, inv2 = ln_stats(resid)
    mlp_in = (normed2 * gain2 + shift2).astype(BF)
    mlp_full = gather_z(mlp_in)
    pre = mm(mlp_full, up_full) + up_shift
    act, slope = gelu_parts(pre)
    hidden = act.astype(BF)

    position = lax.broadcasted_iota(jnp.int32, (total_rows, 1), 0)
    g_full = g_full * (position < length).astype(BF)
    own_position = first + lax.broadcasted_iota(jnp.int32, (rows, 1), 0)
    grad_out = cotangent[0].astype(F32) * (own_position < length).astype(F32)
    grad_pre = mm(g_full, down_t) * slope
    grad_pre_b = grad_pre.astype(BF)
    grad_mlp = scatter_z(mm(grad_pre_b, up_full, NT).astype(BF))
    mlp_part, _ = lax.optimization_barrier((mm(hidden, down_t, NT).astype(BF), grad_mlp))
    mlp_out = scatter_z(mlp_part)
    up_b_block = jnp.sum(grad_pre, axis=0)
    up_dw = mm(mlp_full, grad_pre_b, TN).astype(BF).reshape(n, share, ff)
    down_dw = mm(g_full, hidden, TN).astype(BF).reshape(n, share, ff)

    grad_resid = grad_out + ln_back(grad_mlp, normed2, inv2, gain2)
    grad_resid_b = grad_resid.astype(BF)
    grad_ctx = pad_cols(mm(grad_resid_b, wo, NT).astype(BF), wide)
    dwo = scatter_dp([mm(ctx, grad_resid_b, TN).astype(BF).reshape(n, share, width)])
    dq, dkv = attend_back(meta, q, kv, lse, grad_ctx)
    mlp_dw = scatter_dp([up_dw, down_dw])
    dq, dkv, mlp_out = lax.optimization_barrier((dq, dkv, mlp_out))
    outputs = (resid + mlp_out + bias_d).astype(BF)
    up_grad = mlp_dw[:, :ff]
    down_grad = mlp_dw[:, ff:].T
    dwq = mm(attn_own, dq, TN).astype(BF).reshape(n, share, wide)
    dwkv = mm(attn_full, dkv, TN).astype(BF).reshape(n, share, 2 * wide)
    dw_a = [dwq[:, :cut], dwkv[:, :cut]]
    dw_b = [dwq[:, cut:], dwkv[:, cut:]]
    dq, dkv, send_a, send_b = lax.optimization_barrier(
        (dq, dkv, core_half(dw_a, False), core_half(dw_b, False))
    )
    dw_parts = [scatter_dp(dw_a, send_a), scatter_dp(dw_b, send_b)]
    part_kv = mm(dkv, wkv, NT)
    part_q = mm(dq, wq, NT)
    grad_attn = scatter_z(part_kv.astype(BF))

    dv_sum = pair_split(jnp.sum(dkv.astype(F32), axis=0))[1][:width]
    vec = jnp.stack(
        [
            jnp.sum(part_kv * normed1_full, axis=0) + jnp.sum(part_q * normed1, axis=0),
            jnp.sum(part_kv, axis=0) + jnp.sum(part_q, axis=0),
            jnp.sum(dq.astype(F32), axis=0)[:width],
            dv_sum,
            jnp.sum(grad_resid, axis=0),
            jnp.sum(grad_mlp * normed2, axis=0),
            jnp.sum(grad_mlp, axis=0),
            jnp.sum(grad_out, axis=0),
        ]
    )
    up_b = lax.dynamic_update_slice_in_dim(jnp.zeros((ff_total,), F32), up_b_block, z * ff, 0)
    thin_grad = jnp.concatenate(
        [vec.reshape(8, n, share).transpose(1, 0, 2).reshape(n, 8 * share), up_b.reshape(n, ff_total // n)],
        axis=1,
    )
    thin_len = thin_grad.shape[1]
    thin_grad = scatter_dp([thin_grad.astype(BF)[:, None, :]])

    piece = qkv_cols + width // zs
    dwo = dwo.astype(BF)
    extra = -(-thin_len // piece)
    thin_rows = pad_cols(thin_grad.astype(BF), extra * piece).reshape(extra, piece)
    sums = []
    for part, lo, hi in ((dw_parts[0], 0, cut), (dw_parts[1], cut, share)):
        part = part.astype(BF)
        dwk, dwv = pair_split(part[:, wide:])
        cols = jnp.concatenate([part[:, :width], dwk[:, :width], dwv[:, :width]], axis=1)
        blocks = []
        for j in range(zs):
            out_part = dwo[lo:hi, j * (width // zs) : (j + 1) * (width // zs)]
            blocks.append(jnp.concatenate([cols[:, j * qkv_cols : (j + 1) * qkv_cols], out_part], axis=1))
            if lo:
                lines = -(-(hi - lo + extra) // 16) * 16
                blocks.append(jnp.pad(thin_rows, [(0, lines - (hi - lo) - extra), (0, 0)]))
        block = jnp.concatenate(blocks, axis=0)
        if lo:
            block, grad_attn = lax.optimization_barrier((block, grad_attn))
        sums.append(scatter_z(block))
    input_grad = grad_resid + ln_back(grad_attn + part_q, normed1, inv1, gain1)
    attn_dw = jnp.concatenate([sums[0], sums[1][: share - cut]], axis=0)
    thin_grad = sums[1][share - cut : share - cut + extra].reshape(extra * piece)[:thin_len]
    vec_out = thin_grad[: 8 * share].reshape(8, share)
    return (
        outputs[None],
        input_grad[None],
        vec_out[0],
        vec_out[1],
        attn_dw[:, :qkv_cols],
        vec_out[2],
        vec_out[3],
        attn_dw[:, qkv_cols:],
        vec_out[4],
        vec_out[5],
        vec_out[6],
        up_grad,
        thin_grad[8 * share:],
        down_grad,
        vec_out[7],
    )


def solution(mesh):
    row = P("dp", "seq", None)
    vec = P("dp")
    mat = P("dp", "seq")
    in_specs = (row, vec, row, vec, vec, mat, vec, vec, mat, vec, vec, vec, mat, vec, P("seq", "dp"), vec)
    out_specs = (row, row, vec, vec, mat, vec, vec, mat, vec, vec, vec, mat, vec, P("seq", "dp"), vec)

    return jax.shard_map(shards, mesh=mesh, in_specs=in_specs, out_specs=out_specs, check_vma=False)
```

```python
import jax
import jax.numpy as jnp
from jax import lax
from jax.experimental import pallas as pl
from jax.experimental.pallas import tpu as pltpu
from jax.sharding import PartitionSpec as P


HD = 64
LANES = 128
EPS = 1e-05
GELU_C = 0.7978845608028654
MASKED = -1e30
BF = jnp.bfloat16
F32 = jnp.float32


def mm(a, b, dims=((1,), (0,))):
    return lax.dot_general(a, b, (dims, ((), ())), preferred_element_type=F32)


NT = ((1,), (1,))
TN = ((0,), (0,))


def ln_stats(x):
    average = jnp.mean(x, axis=-1, keepdims=True)
    centered = x - average
    variance = jnp.mean(centered * centered, axis=-1, keepdims=True)
    inv = lax.rsqrt(variance + EPS)
    return centered * inv, inv


def ln_back(grad_in, normed, inv, gain):
    scaled = grad_in * gain
    return inv * (
        scaled
        - jnp.mean(scaled, axis=-1, keepdims=True)
        - normed * jnp.mean(scaled * normed, axis=-1, keepdims=True)
    )


def gelu_parts(pre):
    tangent = jnp.tanh(GELU_C * (pre + 0.044715 * pre * pre * pre))
    result = 0.5 * pre * (1.0 + tangent)
    slope = 0.5 * (1.0 + tangent) + 0.5 * pre * (1.0 - tangent * tangent) * GELU_C * (
        1.0 + 3.0 * 0.044715 * pre * pre
    )
    return result, slope


def head_mask(rows, which):
    lane = lax.broadcasted_iota(jnp.int32, (rows, LANES), 1)
    return (lane >= HD) if which else (lane < HD)


def fill_mask(meta, mask_ref):
    key = lax.broadcasted_iota(jnp.int32, mask_ref.shape, 0)
    row = lax.broadcasted_iota(jnp.int32, mask_ref.shape, 1) + meta[0]
    mask_ref[...] = jnp.where((key <= row) & (key < meta[1]), 0.0, MASKED)


def attend_kernel(meta, q_ref, kv_ref, ctx_ref, lse_ref, mask_ref):
    rows = q_ref.shape[0]

    @pl.when(pl.program_id(0) == 0)
    def _():
        fill_mask(meta, mask_ref)

    k = kv_ref[:, :LANES]
    vt = kv_ref[:, LANES:].T
    q = q_ref[...] * jnp.asarray(HD ** -0.5, BF)
    pieces = []
    for which in range(2):
        qm = jnp.where(head_mask(rows, which), q, jnp.zeros_like(q))
        s = mm(k, qm, NT) + mask_ref[...]
        top = jnp.max(s, axis=0, keepdims=True)
        e = jnp.exp(s - top)
        total = jnp.sum(e, axis=0, keepdims=True)
        weights = (e * (1.0 / total)).astype(BF)
        pieces.append(mm(vt[which * HD:(which + 1) * HD], weights))
        lse_ref[0, which:which + 1, :] = top + jnp.log(total)
    ctx_ref[...] = jnp.concatenate(pieces, axis=0).T.astype(BF)


def attend(meta, q, kv):
    rows, width = q.shape
    keys = kv.shape[0]
    pairs = width // LANES
    return pl.pallas_call(
        attend_kernel,
        grid_spec=pltpu.PrefetchScalarGridSpec(
            num_scalar_prefetch=1,
            grid=(pairs,),
            in_specs=[
                pl.BlockSpec((rows, LANES), lambda p, m: (0, p)),
                pl.BlockSpec((keys, 2 * LANES), lambda p, m: (0, p)),
            ],
            out_specs=[
                pl.BlockSpec((rows, LANES), lambda p, m: (0, p)),
                pl.BlockSpec((1, 2, rows), lambda p, m: (p, 0, 0)),
            ],
            scratch_shapes=[pltpu.VMEM((keys, rows), F32)],
        ),
        out_shape=[
            jax.ShapeDtypeStruct((rows, width), BF),
            jax.ShapeDtypeStruct((pairs, 2, rows), F32),
        ],
        cost_estimate=pl.CostEstimate(
            flops=8 * rows * keys * width, transcendentals=2 * pairs * rows * keys, bytes_accessed=6 * keys * width
        ),
        name="attend",
    )(meta, q, kv)


def attend_back_kernel(meta, q_ref, kv_ref, lse_ref, g_ref, dq_ref, dkv_ref, mask_ref):
    rows = q_ref.shape[0]

    @pl.when(pl.program_id(0) == 0)
    def _():
        fill_mask(meta, mask_ref)

    scale = jnp.asarray(HD ** -0.5, BF)
    k = kv_ref[:, :LANES]
    v = kv_ref[:, LANES:]
    kt = k.T
    q = q_ref[...]
    g = g_ref[...]
    dq, weights_all, ds_all, q_all, g_all = [], [], [], [], []
    for which in range(2):
        mask = head_mask(rows, which)
        qm = jnp.where(mask, q, jnp.zeros_like(q))
        gm = jnp.where(mask, g, jnp.zeros_like(g))
        s = mm(k, qm * scale, NT) + mask_ref[...]
        weights = jnp.exp(s - lse_ref[0, which:which + 1, :])
        dprob = mm(v, gm * scale, NT)
        delta = jnp.sum(weights * dprob, axis=0, keepdims=True)
        ds = (weights * (dprob - delta)).astype(BF)
        dq.append(mm(kt[which * HD:(which + 1) * HD], ds))
        weights_all.append(weights.astype(BF))
        ds_all.append(ds)
        q_all.append(qm)
        g_all.append(gm)
    dq_ref[...] = jnp.concatenate(dq, axis=0).T.astype(BF)
    dk = mm(jnp.concatenate(ds_all, axis=1), jnp.concatenate(q_all, axis=0))
    dv = mm(jnp.concatenate(weights_all, axis=1), jnp.concatenate(g_all, axis=0))
    dkv_ref[:, :LANES] = dk.astype(BF)
    dkv_ref[:, LANES:] = dv.astype(BF)


def attend_back(meta, q, kv, lse, g):
    rows, width = q.shape
    keys = kv.shape[0]
    pairs = width // LANES
    return pl.pallas_call(
        attend_back_kernel,
        grid_spec=pltpu.PrefetchScalarGridSpec(
            num_scalar_prefetch=1,
            grid=(pairs,),
            in_specs=[
                pl.BlockSpec((rows, LANES), lambda p, m: (0, p)),
                pl.BlockSpec((keys, 2 * LANES), lambda p, m: (0, p)),
                pl.BlockSpec((1, 2, rows), lambda p, m: (p, 0, 0)),
                pl.BlockSpec((rows, LANES), lambda p, m: (0, p)),
            ],
            out_specs=[
                pl.BlockSpec((rows, LANES), lambda p, m: (0, p)),
                pl.BlockSpec((keys, 2 * LANES), lambda p, m: (0, p)),
            ],
            scratch_shapes=[pltpu.VMEM((keys, rows), F32)],
        ),
        out_shape=[
            jax.ShapeDtypeStruct((rows, width), BF),
            jax.ShapeDtypeStruct((keys, 2 * width), BF),
        ],
        cost_estimate=pl.CostEstimate(
            flops=20 * rows * keys * width, transcendentals=2 * pairs * rows * keys, bytes_accessed=12 * keys * width
        ),
        name="attend_back",
    )(meta, q, kv, lse, g)


def swap(x, bit):
    n = lax.axis_size("dp")
    return lax.ppermute(x, "dp", [(i, i ^ bit) for i in range(n)])


def ring_z(x):
    size = lax.axis_size("seq")
    me = lax.axis_index("seq")
    parts = [x]
    for d in range(1, size):
        parts.append(lax.ppermute(x, "seq", [(i, (i + d) % size) for i in range(size)]))
    blocks = []
    for j in range(size):
        block = parts[0]
        for d in range(1, size):
            block = jnp.where((me - j) % size == d, parts[d], block)
        blocks.append(block)
    return blocks


def place_kernel(meta, *refs):
    pieces, out, sems = refs[:-2], refs[-2], refs[-1]
    count = out.shape[0]
    copies = []
    at = 0
    for c in range(len(pieces) // count):
        rows = pieces[c * count].shape[0]
        for e in range(count):
            piece = pieces[c * count + e]
            spot = out.at[meta[0] ^ e, pl.ds(at, rows), :]
            copies.append(pltpu.make_async_copy(piece, spot, sems.at[c * count + e]))
        at += rows
    for copy in copies:
        copy.start()
    for copy in copies:
        copy.wait()


def place(me, pieces, count, rows):
    return pl.pallas_call(
        place_kernel,
        grid_spec=pltpu.PrefetchScalarGridSpec(
            num_scalar_prefetch=1,
            grid=(1,),
            in_specs=[pl.BlockSpec(memory_space=pltpu.VMEM)] * len(pieces),
            out_specs=pl.BlockSpec(memory_space=pl.ANY),
            scratch_shapes=[pltpu.SemaphoreType.DMA((len(pieces),))],
        ),
        out_shape=jax.ShapeDtypeStruct((count, rows, pieces[0].shape[1]), pieces[0].dtype),
        name="place",
    )(me.reshape(1).astype(jnp.int32), *pieces)


def gather_dp(chunks, after=None):
    n = lax.axis_size("dp")
    if n != 8:
        full = lax.all_gather(jnp.concatenate(chunks, axis=0), "dp", axis=0)
        return full if after is None else (full, after)
    pieces = []
    for x in chunks:
        for d in range(n // 2):
            got = swap(x, 2 * d) if d else x
            pieces += [got, swap(got, 1)]
    if after is not None:
        pieces[-1], after = lax.optimization_barrier((pieces[-1], after))
    full = place(lax.axis_index("dp"), pieces, n, sum(x.shape[0] for x in chunks))
    return full if after is None else (full, after)


def core_half(grads, mine):
    n = lax.axis_size("dp")
    core = lax.axis_index("dp") % 2
    which = core if mine else 1 - core
    cut_out = [
        lax.dynamic_index_in_dim(g.reshape((n // 2, 2) + g.shape[1:]), which, 1, keepdims=False) for g in grads
    ]
    return jnp.concatenate(cut_out, axis=2)


def scatter_dp(grads, send=None):
    return spread(core_sum(grads, send))


def core_sum(grads, send=None):
    if lax.axis_size("dp") != 8:
        return jnp.concatenate(grads, axis=2)
    got = swap(core_half(grads, False) if send is None else send, 1)
    return (core_half(grads, True).astype(F32) + got.astype(F32)).astype(BF)


def spread(summed):
    n = lax.axis_size("dp")
    if n != 8:
        return lax.psum_scatter(summed, "dp", scatter_dimension=0).astype(F32)
    group = lax.axis_index("dp") // 2
    total = lax.dynamic_index_in_dim(summed, group, 0, keepdims=False).astype(F32)
    for d in range(1, n // 2):
        part = lax.dynamic_index_in_dim(summed, group ^ d, 0, keepdims=False)
        total = total + swap(part, 2 * d).astype(F32)
    return total


def gather_z(x):
    return lax.all_gather(x, "seq", axis=0, tiled=True)


def scatter_z(x):
    return lax.psum_scatter(x, "seq", scatter_dimension=0, tiled=True).astype(F32)


def pad_cols(x, width):
    return jnp.pad(x, [(0, 0)] * (x.ndim - 1) + [(0, width - x.shape[-1])])


def pair_up(a, b):
    lead = a.shape[:-1]
    blocks = a.shape[-1] // LANES
    both = jnp.stack([a.reshape(lead + (blocks, LANES)), b.reshape(lead + (blocks, LANES))], axis=-2)
    return both.reshape(lead + (2 * a.shape[-1],))


def pair_split(x):
    lead = x.shape[:-1]
    both = x.reshape(lead + (x.shape[-1] // (2 * LANES), 2, LANES))
    half = lead + (x.shape[-1] // 2,)
    return both[..., 0, :].reshape(half), both[..., 1, :].reshape(half)


def shards(
    inputs,
    lengths,
    cotangent,
    norm1_gain,
    norm1_bias,
    qkv_weight,
    query_bias,
    value_bias,
    out_weight,
    out_bias,
    norm2_gain,
    norm2_bias,
    up_weight,
    up_bias,
    down_weight,
    down_bias,
):
    n = lax.axis_size("dp")
    zs = lax.axis_size("seq")
    z = lax.axis_index("seq")
    rows, width = inputs.shape[1:]
    total_rows = rows * zs
    share = norm1_gain.shape[0]
    wide = -(-width // LANES) * LANES
    qkv_cols = qkv_weight.shape[1]
    ff = up_weight.shape[1]
    ff_total = ff * zs
    length = lengths[0]
    first = z * rows
    meta = jnp.stack([first, length]).astype(jnp.int32)

    thin = jnp.stack(
        [norm1_gain, norm1_bias, query_bias, value_bias, out_bias, norm2_gain, norm2_bias, down_bias]
    ).reshape(1, 8 * share)
    thin_all = gather_dp([jnp.concatenate([thin, up_bias.reshape(1, -1)], axis=1)])
    thin_all = thin_all.reshape(n, 8 * share + up_bias.shape[0])
    cut = -(-share // 16) * 8
    raw = ring_z(qkv_weight)
    raw, own_x, thin_all = lax.optimization_barrier((raw, inputs[0], thin_all))
    vectors = (
        thin_all[:, : 8 * share].reshape(n, 8, share).transpose(1, 0, 2).reshape(8, width).astype(F32)
    )
    up_bias_all = thin_all[:, 8 * share:].reshape(ff_total).astype(F32)
    gain1, shift1, bias_q, bias_v, bias_o, gain2, shift2, bias_d = [vectors[i] for i in range(8)]
    up_shift = lax.dynamic_slice_in_dim(up_bias_all, z * ff, ff)
    x_full = gather_z(own_x)
    raw = jnp.concatenate(raw, axis=1)
    wq_s = pad_cols(raw[:, :width], wide)
    wk_s = pad_cols(raw[:, width : 2 * width], wide)
    wv_s = pad_cols(raw[:, 2 * width :], wide)
    qkv_s = jnp.concatenate([wq_s, pair_up(wk_s, wv_s)], axis=1)
    x_wide = x_full.astype(F32)
    mean_full = jnp.mean(x_wide, axis=-1, keepdims=True)
    inv_full = lax.rsqrt(jnp.mean((x_wide - mean_full) * (x_wide - mean_full), axis=-1, keepdims=True) + EPS)
    qkv_full, (mean_full, inv_full) = gather_dp([qkv_s], (mean_full, inv_full))
    normed1_full = (x_wide - mean_full) * inv_full
    qkv_full = qkv_full.reshape(width, 3 * wide)
    cot, qkv_full = lax.optimization_barrier((cotangent[0], qkv_full))
    g_full = gather_z(cot)
    out_rows = jnp.concatenate(ring_z(out_weight), axis=1)
    out_rows, up_s, down_s, qkv_full = lax.optimization_barrier((out_rows, up_weight, down_weight, qkv_full))
    wq = qkv_full[:, :wide]
    wkv = qkv_full[:, wide:]

    x_own = inputs[0].astype(F32)
    normed1, inv1 = ln_stats(x_own)
    attn_own = (normed1 * gain1 + shift1).astype(BF)
    attn_full = (normed1_full * gain1 + shift1).astype(BF)
    q = (mm(attn_own, wq) + pad_cols(bias_q, wide)).astype(BF)
    bias_kv = pair_up(jnp.zeros((wide,), F32), pad_cols(bias_v, wide))
    kv = (mm(attn_full, wkv) + bias_kv).astype(BF)
    wo = gather_dp([out_rows]).reshape(width, width)
    mlp_w = gather_dp([jnp.concatenate([up_s, down_s.T], axis=1)]).reshape(width, 2 * ff)
    up_full = mlp_w[:, :ff]
    down_t = mlp_w[:, ff:]
    ctx, lse = attend(meta, q, kv)
    ctx, g_full = lax.optimization_barrier((ctx, g_full))
    ctx = ctx[:, :width]
    resid = x_own + mm(ctx, wo) + bias_o
    normed2, inv2 = ln_stats(resid)
    mlp_in = (normed2 * gain2 + shift2).astype(BF)
    mlp_full = gather_z(mlp_in)
    pre = mm(mlp_full, up_full) + up_shift
    act, slope = gelu_parts(pre)
    hidden = act.astype(BF)

    position = lax.broadcasted_iota(jnp.int32, (total_rows, 1), 0)
    g_full = g_full * (position < length).astype(BF)
    own_position = first + lax.broadcasted_iota(jnp.int32, (rows, 1), 0)
    grad_out = cotangent[0].astype(F32) * (own_position < length).astype(F32)
    grad_pre = mm(g_full, down_t) * slope
    grad_pre_b = grad_pre.astype(BF)
    grad_mlp = scatter_z(mm(grad_pre_b, up_full, NT).astype(BF))
    mlp_part, _ = lax.optimization_barrier((mm(hidden, down_t, NT).astype(BF), grad_mlp))
    mlp_out = scatter_z(mlp_part)
    up_b_block = jnp.sum(grad_pre, axis=0)
    up_dw = mm(mlp_full, grad_pre_b, TN).astype(BF).reshape(n, share, ff)
    down_dw = mm(g_full, hidden, TN).astype(BF).reshape(n, share, ff)

    grad_resid = grad_out + ln_back(grad_mlp, normed2, inv2, gain2)
    grad_resid_b = grad_resid.astype(BF)
    grad_ctx = pad_cols(mm(grad_resid_b, wo, NT).astype(BF), wide)
    dwo = scatter_dp([mm(ctx, grad_resid_b, TN).astype(BF).reshape(n, share, width)])
    dq, dkv = attend_back(meta, q, kv, lse, grad_ctx)
    mlp_dw = scatter_dp([up_dw, down_dw])
    dq, dkv, mlp_out = lax.optimization_barrier((dq, dkv, mlp_out))
    outputs = (resid + mlp_out + bias_d).astype(BF)
    up_grad = mlp_dw[:, :ff]
    down_grad = mlp_dw[:, ff:].T
    dwq = mm(attn_own, dq, TN).astype(BF).reshape(n, share, wide)
    dwkv = mm(attn_full, dkv, TN).astype(BF).reshape(n, share, 2 * wide)
    dw_a = [dwq[:, :cut], dwkv[:, :cut]]
    dw_b = [dwq[:, cut:], dwkv[:, cut:]]
    dq, dkv, send_a, send_b = lax.optimization_barrier(
        (dq, dkv, core_half(dw_a, False), core_half(dw_b, False))
    )
    sum_a = core_sum(dw_a, send_a)
    sum_b = core_sum(dw_b, send_b)
    part_kv = mm(dkv, wkv, NT)
    part_b, part_kv = lax.optimization_barrier((part_kv.astype(BF), part_kv))
    part_q = mm(dq, wq, NT)
    grad_attn = scatter_z(part_b)
    part_kv, part_q, dq, dkv, sum_a, sum_b = lax.optimization_barrier((part_kv, part_q, dq, dkv, sum_a, sum_b))
    dw_parts = [spread(sum_a), spread(sum_b)]

    dv_sum = pair_split(jnp.sum(dkv.astype(F32), axis=0))[1][:width]
    vec = jnp.stack(
        [
            jnp.sum(part_kv * normed1_full, axis=0) + jnp.sum(part_q * normed1, axis=0),
            jnp.sum(part_kv, axis=0) + jnp.sum(part_q, axis=0),
            jnp.sum(dq.astype(F32), axis=0)[:width],
            dv_sum,
            jnp.sum(grad_resid, axis=0),
            jnp.sum(grad_mlp * normed2, axis=0),
            jnp.sum(grad_mlp, axis=0),
            jnp.sum(grad_out, axis=0),
        ]
    )
    up_b = lax.dynamic_update_slice_in_dim(jnp.zeros((ff_total,), F32), up_b_block, z * ff, 0)
    thin_grad = jnp.concatenate(
        [vec.reshape(8, n, share).transpose(1, 0, 2).reshape(n, 8 * share), up_b.reshape(n, ff_total // n)],
        axis=1,
    )
    thin_len = thin_grad.shape[1]
    thin_grad = scatter_dp([thin_grad.astype(BF)[:, None, :]])

    piece = qkv_cols + width // zs
    dwo = dwo.astype(BF)
    extra = -(-thin_len // piece)
    thin_rows = pad_cols(thin_grad.astype(BF), extra * piece).reshape(extra, piece)
    sums = []
    for part, lo, hi in ((dw_parts[0], 0, cut), (dw_parts[1], cut, share)):
        part = part.astype(BF)
        dwk, dwv = pair_split(part[:, wide:])
        cols = jnp.concatenate([part[:, :width], dwk[:, :width], dwv[:, :width]], axis=1)
        blocks = []
        for j in range(zs):
            out_part = dwo[lo:hi, j * (width // zs) : (j + 1) * (width // zs)]
            blocks.append(jnp.concatenate([cols[:, j * qkv_cols : (j + 1) * qkv_cols], out_part], axis=1))
            if lo:
                lines = -(-(hi - lo + extra) // 16) * 16
                blocks.append(jnp.pad(thin_rows, [(0, lines - (hi - lo) - extra), (0, 0)]))
        block = jnp.concatenate(blocks, axis=0)
        if lo:
            block, grad_attn = lax.optimization_barrier((block, grad_attn))
        sums.append(scatter_z(block))
    input_grad = grad_resid + ln_back(grad_attn + part_q, normed1, inv1, gain1)
    attn_dw = jnp.concatenate([sums[0], sums[1][: share - cut]], axis=0)
    thin_grad = sums[1][share - cut : share - cut + extra].reshape(extra * piece)[:thin_len]
    vec_out = thin_grad[: 8 * share].reshape(8, share)
    return (
        outputs[None],
        input_grad[None],
        vec_out[0],
        vec_out[1],
        attn_dw[:, :qkv_cols],
        vec_out[2],
        vec_out[3],
        attn_dw[:, qkv_cols:],
        vec_out[4],
        vec_out[5],
        vec_out[6],
        up_grad,
        thin_grad[8 * share:],
        down_grad,
        vec_out[7],
    )


def solution(mesh):
    row = P("dp", "seq", None)
    vec = P("dp")
    mat = P("dp", "seq")
    in_specs = (row, vec, row, vec, vec, mat, vec, vec, mat, vec, vec, vec, mat, vec, P("seq", "dp"), vec)
    out_specs = (row, row, vec, vec, mat, vec, vec, mat, vec, vec, vec, mat, vec, P("seq", "dp"), vec)

    return jax.shard_map(shards, mesh=mesh, in_specs=in_specs, out_specs=out_specs, check_vma=False)
```

```python
import jax
import jax.numpy as jnp
from jax import lax
from jax.experimental import pallas as pl
from jax.experimental.pallas import tpu as pltpu
from jax.sharding import PartitionSpec as P


HD = 64
LANES = 128
EPS = 1e-05
GELU_C = 0.7978845608028654
MASKED = -1e30
BF = jnp.bfloat16
F32 = jnp.float32


def mm(a, b, dims=((1,), (0,))):
    return lax.dot_general(a, b, (dims, ((), ())), preferred_element_type=F32)


NT = ((1,), (1,))
TN = ((0,), (0,))


def ln_stats(x):
    average = jnp.mean(x, axis=-1, keepdims=True)
    centered = x - average
    variance = jnp.mean(centered * centered, axis=-1, keepdims=True)
    inv = lax.rsqrt(variance + EPS)
    return centered * inv, inv


def ln_back(grad_in, normed, inv, gain):
    scaled = grad_in * gain
    return inv * (
        scaled
        - jnp.mean(scaled, axis=-1, keepdims=True)
        - normed * jnp.mean(scaled * normed, axis=-1, keepdims=True)
    )


def gelu_parts(pre):
    tangent = jnp.tanh(GELU_C * (pre + 0.044715 * pre * pre * pre))
    result = 0.5 * pre * (1.0 + tangent)
    slope = 0.5 * (1.0 + tangent) + 0.5 * pre * (1.0 - tangent * tangent) * GELU_C * (
        1.0 + 3.0 * 0.044715 * pre * pre
    )
    return result, slope


def head_mask(rows, which):
    lane = lax.broadcasted_iota(jnp.int32, (rows, LANES), 1)
    return (lane >= HD) if which else (lane < HD)


def fill_mask(meta, mask_ref):
    key = lax.broadcasted_iota(jnp.int32, mask_ref.shape, 0)
    row = lax.broadcasted_iota(jnp.int32, mask_ref.shape, 1) + meta[0]
    mask_ref[...] = jnp.where((key <= row) & (key < meta[1]), 0.0, MASKED)


def attend_kernel(meta, q_ref, kv_ref, ctx_ref, lse_ref, mask_ref):
    rows = q_ref.shape[0]

    @pl.when(pl.program_id(0) == 0)
    def _():
        fill_mask(meta, mask_ref)

    k = kv_ref[:, :LANES]
    vt = kv_ref[:, LANES:].T
    q = q_ref[...] * jnp.asarray(HD ** -0.5, BF)
    pieces = []
    for which in range(2):
        qm = jnp.where(head_mask(rows, which), q, jnp.zeros_like(q))
        s = mm(k, qm, NT) + mask_ref[...]
        top = jnp.max(s, axis=0, keepdims=True)
        e = jnp.exp(s - top)
        total = jnp.sum(e, axis=0, keepdims=True)
        weights = (e * (1.0 / total)).astype(BF)
        pieces.append(mm(vt[which * HD:(which + 1) * HD], weights))
        lse_ref[0, which:which + 1, :] = top + jnp.log(total)
    ctx_ref[...] = jnp.concatenate(pieces, axis=0).T.astype(BF)


def attend(meta, q, kv):
    rows, width = q.shape
    keys = kv.shape[0]
    pairs = width // LANES
    return pl.pallas_call(
        attend_kernel,
        grid_spec=pltpu.PrefetchScalarGridSpec(
            num_scalar_prefetch=1,
            grid=(pairs,),
            in_specs=[
                pl.BlockSpec((rows, LANES), lambda p, m: (0, p)),
                pl.BlockSpec((keys, 2 * LANES), lambda p, m: (0, p)),
            ],
            out_specs=[
                pl.BlockSpec((rows, LANES), lambda p, m: (0, p)),
                pl.BlockSpec((1, 2, rows), lambda p, m: (p, 0, 0)),
            ],
            scratch_shapes=[pltpu.VMEM((keys, rows), F32)],
        ),
        out_shape=[
            jax.ShapeDtypeStruct((rows, width), BF),
            jax.ShapeDtypeStruct((pairs, 2, rows), F32),
        ],
        cost_estimate=pl.CostEstimate(
            flops=8 * rows * keys * width, transcendentals=2 * pairs * rows * keys, bytes_accessed=6 * keys * width
        ),
        name="attend",
    )(meta, q, kv)


def attend_back_kernel(meta, q_ref, kv_ref, lse_ref, g_ref, dq_ref, dkv_ref, mask_ref):
    rows = q_ref.shape[0]

    @pl.when(pl.program_id(0) == 0)
    def _():
        fill_mask(meta, mask_ref)

    scale = jnp.asarray(HD ** -0.5, BF)
    k = kv_ref[:, :LANES]
    v = kv_ref[:, LANES:]
    kt = k.T
    q = q_ref[...]
    g = g_ref[...]
    dq, weights_all, ds_all, q_all, g_all = [], [], [], [], []
    for which in range(2):
        mask = head_mask(rows, which)
        qm = jnp.where(mask, q, jnp.zeros_like(q))
        gm = jnp.where(mask, g, jnp.zeros_like(g))
        s = mm(k, qm * scale, NT) + mask_ref[...]
        weights = jnp.exp(s - lse_ref[0, which:which + 1, :])
        dprob = mm(v, gm * scale, NT)
        delta = jnp.sum(weights * dprob, axis=0, keepdims=True)
        ds = (weights * (dprob - delta)).astype(BF)
        dq.append(mm(kt[which * HD:(which + 1) * HD], ds))
        weights_all.append(weights.astype(BF))
        ds_all.append(ds)
        q_all.append(qm)
        g_all.append(gm)
    dq_ref[...] = jnp.concatenate(dq, axis=0).T.astype(BF)
    dk = mm(jnp.concatenate(ds_all, axis=1), jnp.concatenate(q_all, axis=0))
    dv = mm(jnp.concatenate(weights_all, axis=1), jnp.concatenate(g_all, axis=0))
    dkv_ref[:, :LANES] = dk.astype(BF)
    dkv_ref[:, LANES:] = dv.astype(BF)


def attend_back(meta, q, kv, lse, g):
    rows, width = q.shape
    keys = kv.shape[0]
    pairs = width // LANES
    return pl.pallas_call(
        attend_back_kernel,
        grid_spec=pltpu.PrefetchScalarGridSpec(
            num_scalar_prefetch=1,
            grid=(pairs,),
            in_specs=[
                pl.BlockSpec((rows, LANES), lambda p, m: (0, p)),
                pl.BlockSpec((keys, 2 * LANES), lambda p, m: (0, p)),
                pl.BlockSpec((1, 2, rows), lambda p, m: (p, 0, 0)),
                pl.BlockSpec((rows, LANES), lambda p, m: (0, p)),
            ],
            out_specs=[
                pl.BlockSpec((rows, LANES), lambda p, m: (0, p)),
                pl.BlockSpec((keys, 2 * LANES), lambda p, m: (0, p)),
            ],
            scratch_shapes=[pltpu.VMEM((keys, rows), F32)],
        ),
        out_shape=[
            jax.ShapeDtypeStruct((rows, width), BF),
            jax.ShapeDtypeStruct((keys, 2 * width), BF),
        ],
        cost_estimate=pl.CostEstimate(
            flops=20 * rows * keys * width, transcendentals=2 * pairs * rows * keys, bytes_accessed=12 * keys * width
        ),
        name="attend_back",
    )(meta, q, kv, lse, g)


def swap(x, bit):
    n = lax.axis_size("dp")
    return lax.ppermute(x, "dp", [(i, i ^ bit) for i in range(n)])


def ring_z(x):
    size = lax.axis_size("seq")
    me = lax.axis_index("seq")
    parts = [x]
    for d in range(1, size):
        parts.append(lax.ppermute(x, "seq", [(i, (i + d) % size) for i in range(size)]))
    blocks = []
    for j in range(size):
        block = parts[0]
        for d in range(1, size):
            block = jnp.where((me - j) % size == d, parts[d], block)
        blocks.append(block)
    return blocks


def place_kernel(meta, *refs):
    pieces, out, sems = refs[:-2], refs[-2], refs[-1]
    count = out.shape[0]
    copies = []
    at = 0
    for c in range(len(pieces) // count):
        rows = pieces[c * count].shape[0]
        for e in range(count):
            piece = pieces[c * count + e]
            spot = out.at[meta[0] ^ e, pl.ds(at, rows), :]
            copies.append(pltpu.make_async_copy(piece, spot, sems.at[c * count + e]))
        at += rows
    for copy in copies:
        copy.start()
    for copy in copies:
        copy.wait()


def place(me, pieces, count, rows):
    return pl.pallas_call(
        place_kernel,
        grid_spec=pltpu.PrefetchScalarGridSpec(
            num_scalar_prefetch=1,
            grid=(1,),
            in_specs=[pl.BlockSpec(memory_space=pltpu.VMEM)] * len(pieces),
            out_specs=pl.BlockSpec(memory_space=pl.ANY),
            scratch_shapes=[pltpu.SemaphoreType.DMA((len(pieces),))],
        ),
        out_shape=jax.ShapeDtypeStruct((count, rows, pieces[0].shape[1]), pieces[0].dtype),
        name="place",
    )(me.reshape(1).astype(jnp.int32), *pieces)


def gather_dp(chunks, value=None, work=None):
    n = lax.axis_size("dp")
    if n != 8:
        full = lax.all_gather(jnp.concatenate(chunks, axis=0), "dp", axis=0)
        return full if work is None else (full, work(value))
    pieces = []
    for x in chunks:
        for d in range(n // 2):
            got = swap(x, 2 * d) if d else x
            pieces += [got, swap(got, 1)]
    if work is not None:
        pieces[2], pieces[4], pieces[6], value = lax.optimization_barrier((pieces[2], pieces[4], pieces[6], value))
        pieces[-1], done = lax.optimization_barrier((pieces[-1], work(value)))
    full = place(lax.axis_index("dp"), pieces, n, sum(x.shape[0] for x in chunks))
    return full if work is None else (full, done)


def core_half(grads, mine):
    n = lax.axis_size("dp")
    core = lax.axis_index("dp") % 2
    which = core if mine else 1 - core
    cut_out = [
        lax.dynamic_index_in_dim(g.reshape((n // 2, 2) + g.shape[1:]), which, 1, keepdims=False) for g in grads
    ]
    return jnp.concatenate(cut_out, axis=2)


def scatter_dp(grads, send=None):
    n = lax.axis_size("dp")
    if n != 8:
        return lax.psum_scatter(jnp.concatenate(grads, axis=2), "dp", scatter_dimension=0).astype(F32)
    group = lax.axis_index("dp") // 2
    got = swap(core_half(grads, False) if send is None else send, 1)
    summed = (core_half(grads, True).astype(F32) + got.astype(F32)).astype(BF)
    total = lax.dynamic_index_in_dim(summed, group, 0, keepdims=False).astype(F32)
    for d in range(1, n // 2):
        part = lax.dynamic_index_in_dim(summed, group ^ d, 0, keepdims=False)
        total = total + swap(part, 2 * d).astype(F32)
    return total


def gather_z(x):
    return lax.all_gather(x, "seq", axis=0, tiled=True)


def scatter_z(x):
    return lax.psum_scatter(x, "seq", scatter_dimension=0, tiled=True).astype(F32)


def pad_cols(x, width):
    return jnp.pad(x, [(0, 0)] * (x.ndim - 1) + [(0, width - x.shape[-1])])


def pair_up(a, b):
    lead = a.shape[:-1]
    blocks = a.shape[-1] // LANES
    both = jnp.stack([a.reshape(lead + (blocks, LANES)), b.reshape(lead + (blocks, LANES))], axis=-2)
    return both.reshape(lead + (2 * a.shape[-1],))


def pair_split(x):
    lead = x.shape[:-1]
    both = x.reshape(lead + (x.shape[-1] // (2 * LANES), 2, LANES))
    half = lead + (x.shape[-1] // 2,)
    return both[..., 0, :].reshape(half), both[..., 1, :].reshape(half)


def shards(
    inputs,
    lengths,
    cotangent,
    norm1_gain,
    norm1_bias,
    qkv_weight,
    query_bias,
    value_bias,
    out_weight,
    out_bias,
    norm2_gain,
    norm2_bias,
    up_weight,
    up_bias,
    down_weight,
    down_bias,
):
    n = lax.axis_size("dp")
    zs = lax.axis_size("seq")
    z = lax.axis_index("seq")
    rows, width = inputs.shape[1:]
    total_rows = rows * zs
    share = norm1_gain.shape[0]
    wide = -(-width // LANES) * LANES
    qkv_cols = qkv_weight.shape[1]
    ff = up_weight.shape[1]
    ff_total = ff * zs
    length = lengths[0]
    first = z * rows
    meta = jnp.stack([first, length]).astype(jnp.int32)

    thin = jnp.stack(
        [norm1_gain, norm1_bias, query_bias, value_bias, out_bias, norm2_gain, norm2_bias, down_bias]
    ).reshape(1, 8 * share)
    thin_all = gather_dp([jnp.concatenate([thin, up_bias.reshape(1, -1)], axis=1)])
    thin_all = thin_all.reshape(n, 8 * share + up_bias.shape[0])
    cut = -(-share // 16) * 8
    raw = ring_z(qkv_weight)
    raw, own_x, thin_all = lax.optimization_barrier((raw, inputs[0], thin_all))
    vectors = (
        thin_all[:, : 8 * share].reshape(n, 8, share).transpose(1, 0, 2).reshape(8, width).astype(F32)
    )
    up_bias_all = thin_all[:, 8 * share:].reshape(ff_total).astype(F32)
    gain1, shift1, bias_q, bias_v, bias_o, gain2, shift2, bias_d = [vectors[i] for i in range(8)]
    up_shift = lax.dynamic_slice_in_dim(up_bias_all, z * ff, ff)
    x_full = gather_z(own_x)
    raw = jnp.concatenate(raw, axis=1)
    wq_s = pad_cols(raw[:, :width], wide)
    wk_s = pad_cols(raw[:, width : 2 * width], wide)
    wv_s = pad_cols(raw[:, 2 * width :], wide)
    qkv_s = jnp.concatenate([wq_s, pair_up(wk_s, wv_s)], axis=1)

    def row_stats(x):
        x_wide = x.astype(F32)
        mean = jnp.mean(x_wide, axis=-1, keepdims=True)
        inv = lax.rsqrt(jnp.mean((x_wide - mean) * (x_wide - mean), axis=-1, keepdims=True) + EPS)
        return x, mean, inv

    qkv_full, (x_full, mean_full, inv_full) = gather_dp([qkv_s], x_full, row_stats)
    cot, x_full = lax.optimization_barrier((cotangent[0], x_full))
    g_full = gather_z(cot)
    x_wide = x_full.astype(F32)
    normed1_full = (x_wide - mean_full) * inv_full
    qkv_full = qkv_full.reshape(width, 3 * wide)
    out_rows = jnp.concatenate(ring_z(out_weight), axis=1)
    out_rows, qkv_full = lax.optimization_barrier((out_rows, qkv_full))
    wq = qkv_full[:, :wide]
    wkv = qkv_full[:, wide:]

    x_own = inputs[0].astype(F32)
    normed1, inv1 = ln_stats(x_own)
    attn_own = (normed1 * gain1 + shift1).astype(BF)
    attn_full = (normed1_full * gain1 + shift1).astype(BF)
    q = (mm(attn_own, wq) + pad_cols(bias_q, wide)).astype(BF)
    bias_kv = pair_up(jnp.zeros((wide,), F32), pad_cols(bias_v, wide))
    kv = (mm(attn_full, wkv) + bias_kv).astype(BF)
    wo = gather_dp([out_rows]).reshape(width, width)
    ctx, lse = attend(meta, q, kv)
    ctx, g_full = lax.optimization_barrier((ctx, g_full))
    ctx = ctx[:, :width]
    resid = x_own + mm(ctx, wo) + bias_o
    normed2, inv2 = ln_stats(resid)
    mlp_in = (normed2 * gain2 + shift2).astype(BF)
    mlp_full = gather_z(mlp_in)
    up_s, down_s, resid = lax.optimization_barrier((up_weight, down_weight, resid))
    mlp_w = gather_dp([jnp.concatenate([up_s, down_s.T], axis=1)]).reshape(width, 2 * ff)
    up_full = mlp_w[:, :ff]
    down_t = mlp_w[:, ff:]
    pre = mm(mlp_full, up_full) + up_shift
    act, slope = gelu_parts(pre)
    hidden = act.astype(BF)

    position = lax.broadcasted_iota(jnp.int32, (total_rows, 1), 0)
    g_full = g_full * (position < length).astype(BF)
    own_position = first + lax.broadcasted_iota(jnp.int32, (rows, 1), 0)
    grad_out = cotangent[0].astype(F32) * (own_position < length).astype(F32)
    grad_pre = mm(g_full, down_t) * slope
    grad_pre_b = grad_pre.astype(BF)
    grad_mlp = scatter_z(mm(grad_pre_b, up_full, NT).astype(BF))
    mlp_part, _ = lax.optimization_barrier((mm(hidden, down_t, NT).astype(BF), grad_mlp))
    mlp_out = scatter_z(mlp_part)
    up_b_block = jnp.sum(grad_pre, axis=0)
    up_dw = mm(mlp_full, grad_pre_b, TN).astype(BF).reshape(n, share, ff)
    down_dw = mm(g_full, hidden, TN).astype(BF).reshape(n, share, ff)

    grad_resid = grad_out + ln_back(grad_mlp, normed2, inv2, gain2)
    grad_resid_b = grad_resid.astype(BF)
    grad_ctx = pad_cols(mm(grad_resid_b, wo, NT).astype(BF), wide)
    dwo = scatter_dp([mm(ctx, grad_resid_b, TN).astype(BF).reshape(n, share, width)])
    dq, dkv = attend_back(meta, q, kv, lse, grad_ctx)
    mlp_dw = scatter_dp([up_dw, down_dw])
    dq, dkv, mlp_out = lax.optimization_barrier((dq, dkv, mlp_out))
    outputs = (resid + mlp_out + bias_d).astype(BF)
    up_grad = mlp_dw[:, :ff]
    down_grad = mlp_dw[:, ff:].T
    dwq = mm(attn_own, dq, TN).astype(BF).reshape(n, share, wide)
    dwkv = mm(attn_full, dkv, TN).astype(BF).reshape(n, share, 2 * wide)
    dw_a = [dwq[:, :cut], dwkv[:, :cut]]
    dw_b = [dwq[:, cut:], dwkv[:, cut:]]
    dq, dkv, send_a, send_b = lax.optimization_barrier(
        (dq, dkv, core_half(dw_a, False), core_half(dw_b, False))
    )
    dw_parts = [scatter_dp(dw_a, send_a), scatter_dp(dw_b, send_b)]
    part_kv = mm(dkv, wkv, NT)
    part_q = mm(dq, wq, NT)
    grad_attn = scatter_z(part_kv.astype(BF))

    dv_sum = pair_split(jnp.sum(dkv.astype(F32), axis=0))[1][:width]
    vec = jnp.stack(
        [
            jnp.sum(part_kv * normed1_full, axis=0) + jnp.sum(part_q * normed1, axis=0),
            jnp.sum(part_kv, axis=0) + jnp.sum(part_q, axis=0),
            jnp.sum(dq.astype(F32), axis=0)[:width],
            dv_sum,
            jnp.sum(grad_resid, axis=0),
            jnp.sum(grad_mlp * normed2, axis=0),
            jnp.sum(grad_mlp, axis=0),
            jnp.sum(grad_out, axis=0),
        ]
    )
    up_b = lax.dynamic_update_slice_in_dim(jnp.zeros((ff_total,), F32), up_b_block, z * ff, 0)
    thin_grad = jnp.concatenate(
        [vec.reshape(8, n, share).transpose(1, 0, 2).reshape(n, 8 * share), up_b.reshape(n, ff_total // n)],
        axis=1,
    )
    thin_len = thin_grad.shape[1]
    thin_grad = scatter_dp([thin_grad.astype(BF)[:, None, :]])

    piece = qkv_cols + width // zs
    dwo = dwo.astype(BF)
    extra = -(-thin_len // piece)
    thin_rows = pad_cols(thin_grad.astype(BF), extra * piece).reshape(extra, piece)
    sums = []
    for part, lo, hi in ((dw_parts[0], 0, cut), (dw_parts[1], cut, share)):
        part = part.astype(BF)
        dwk, dwv = pair_split(part[:, wide:])
        cols = jnp.concatenate([part[:, :width], dwk[:, :width], dwv[:, :width]], axis=1)
        blocks = []
        for j in range(zs):
            out_part = dwo[lo:hi, j * (width // zs) : (j + 1) * (width // zs)]
            blocks.append(jnp.concatenate([cols[:, j * qkv_cols : (j + 1) * qkv_cols], out_part], axis=1))
            if lo:
                lines = -(-(hi - lo + extra) // 16) * 16
                blocks.append(jnp.pad(thin_rows, [(0, lines - (hi - lo) - extra), (0, 0)]))
        block = jnp.concatenate(blocks, axis=0)
        if lo:
            block, grad_attn = lax.optimization_barrier((block, grad_attn))
        sums.append(scatter_z(block))
    input_grad = grad_resid + ln_back(grad_attn + part_q, normed1, inv1, gain1)
    attn_dw = jnp.concatenate([sums[0], sums[1][: share - cut]], axis=0)
    thin_grad = sums[1][share - cut : share - cut + extra].reshape(extra * piece)[:thin_len]
    vec_out = thin_grad[: 8 * share].reshape(8, share)
    return (
        outputs[None],
        input_grad[None],
        vec_out[0],
        vec_out[1],
        attn_dw[:, :qkv_cols],
        vec_out[2],
        vec_out[3],
        attn_dw[:, qkv_cols:],
        vec_out[4],
        vec_out[5],
        vec_out[6],
        up_grad,
        thin_grad[8 * share:],
        down_grad,
        vec_out[7],
    )


def solution(mesh):
    row = P("dp", "seq", None)
    vec = P("dp")
    mat = P("dp", "seq")
    in_specs = (row, vec, row, vec, vec, mat, vec, vec, mat, vec, vec, vec, mat, vec, P("seq", "dp"), vec)
    out_specs = (row, row, vec, vec, mat, vec, vec, mat, vec, vec, vec, mat, vec, P("seq", "dp"), vec)

    return jax.shard_map(shards, mesh=mesh, in_specs=in_specs, out_specs=out_specs, check_vma=False)
```
